32 devices in a mesh: frame: 8 (over y, x, core), expert: 4 (over z).
Axes of the slice: x: 2, y: 2, z: 4, core: 2. Of those that a mesh axis runs over, the one named last changes fastest.
Arguments:
- patches: bfloat16 [8, 4, 256, 1536], P('frame', 'expert'), may hold values from -6 to 6
- temporal_q: bfloat16 [8, 4, 256, 1536], P('frame', 'expert'), may hold values from -70 to 70
- temporal_k: bfloat16 [8, 4, 256, 1536], P('frame', 'expert'), may hold values from -6 to 6
- temporal_v: bfloat16 [8, 4, 256, 1536], P('frame', 'expert'), may hold values from -6 to 6
- clip_lengths: int32 [4], P('expert'), may hold values from 1 to 8
- w_time: bfloat16 [1536, 1536], replicated, may hold values from -0.15625 to 0.15625
- gain_space: float32 [1536], replicated, may hold values from 0.1 to 1.9
- w_space: bfloat16 [1536, 4608], P(None, 'frame'), may hold values from -2 to 2
- w_merge: bfloat16 [1536, 1536], replicated, may hold values from -0.15625 to 0.15625
- gain_mix: float32 [1536], replicated, may hold values from 0.1 to 1.9
- expert_ids: int32 [8, 4, 256, 2], P('frame', 'expert'), may hold values from 0 to 31, all different within a row; in each aligned block of 256 rows (0 to 255, 256 to 511, ..., all dimensions but the last counted through in order) at most 18 rows name the same one
- gate_weights: float32 [8, 4, 256, 2], P('frame', 'expert'), may hold values from 0.25 to 1
- w_expand: bfloat16 [32, 1536, 6144], P(('frame', 'expert')), may hold values from -0.15625 to 0.15625
- w_reduce: bfloat16 [32, 6144, 1536], P(('frame', 'expert')), may hold values from -0.078125 to 0.078125
Outputs:
- block_out: bfloat16 [8, 4, 256, 1536], P('frame', 'expert')
The draws below stay inside these ranges and needn't reach their ends.
Inputs may be any that keep to these rules, and one draw needn't show every extreme that they name: `expert_ids`: the rows of one device (the 256 rows of one frame and 1 clips) name no expert more than 18 times, and in some device's rows an expert is named exactly 18 times; the two experts of a row differ.
All inputs are finite; a program needn't handle non-finite values.
Results may differ from the reference program's by a relative error of at most 0.0065.
Values may be sent and summed in bfloat16 or wider, within the bound.
A program may use at most 128 MiB of HBM per device.

```python
import math
import jax
import jax.numpy as jnp
import numpy as np
from jax import lax

D = 1536
HEADS = 24
FF_EXPERT = 6144
EXPERTS = 32
PATCHES = 256
FRAMES = 8
CLIPS = 4
ROWS_DEV = 256
CAP = 18
SHARDS = 1
HID_DEV = 6144
DEVICES = 32


def query_key_pair(key):
    full_shape = (FRAMES, CLIPS, PATCHES, D)
    key_rows = jnp.clip(jax.random.normal(jax.random.fold_in(key, 11), full_shape, jnp.float32), -6.0, 6.0)
    queries = jnp.clip(jax.random.normal(jax.random.fold_in(key, 12), full_shape, jnp.float32), -6.0, 6.0)
    return (queries, key_rows)


def draw_temporal_q(key, part):
    return query_key_pair(key)[0].astype(jnp.bfloat16)


def draw_temporal_k(key, part):
    return query_key_pair(key)[1].astype(jnp.bfloat16)


def draw_w_space(key, part):
    factor = D ** (-0.5)
    base = jax.random.normal(jax.random.fold_in(key, 21), (D, 3 * D), jnp.float32) * factor
    return base.astype(jnp.bfloat16)


def plant(array, stream_key, low, largest):
    index_at = [jax.random.randint(jax.random.fold_in(stream_key, axis), (), 0, length) for axis, length in enumerate(array.shape)]
    main_axis = array.shape.index(max(array.shape))
    beside = index_at[:main_axis] + [(index_at[main_axis] + 1) % array.shape[main_axis]] + index_at[main_axis + 1:]
    return array.at[tuple(index_at)].set(low).at[tuple(beside)].set(largest)


def block_scale(stream_key, extent, shards, smallest, largest):
    factor_of, own = 1.0, jax.random.fold_in(stream_key, 6)
    for axis_at, shards_of in shards:
        draws = jnp.exp(jax.random.uniform(jax.random.fold_in(own, axis_at), (shards_of,), jnp.float32, smallest / len(shards), largest / len(shards)))
        factor_of = factor_of * jnp.repeat(draws, extent[axis_at] // shards_of).reshape([-1 if axis == axis_at else 1 for axis in range(len(extent))])
    return factor_of


def routed_block(own_key, own, number, rows, amount, top, most, skew):
    ranking = jax.random.permutation(own_key, amount)
    crowded, usual = portions_of(amount, rows * top, most, skew, True), portions_of(amount, rows * top, most, skew, False)
    places = jnp.arange(amount)

    def named(lengths, rotation):
        used = int((lengths > 0).sum())
        fixed = max(1, used // 4)
        shifted = fixed + (places - fixed + rotation * (used - fixed)) % max(1, amount - fixed)
        return jnp.zeros((amount,), jnp.int32).at[ranking[jnp.where(places < fixed, places, shifted)]].set(jnp.asarray(lengths, jnp.int32))

    lengths = jnp.where(number % 4 == 0, named(crowded, number // 4), named(usual, number - number // 4 - 1))
    mixed = jax.random.permutation(jax.random.fold_in(own, 3), amount)
    giver, sink = mixed[0:amount // 2 * 2:2], mixed[1:amount // 2 * 2:2]
    room = jnp.minimum(lengths[giver] - 1, most - lengths[sink]) // 2
    room = jnp.where((giver == ranking[0]) | (sink == ranking[0]) | (lengths[sink] == 0), 0, jnp.maximum(room, 0))
    shifted = jax.random.randint(jax.random.fold_in(own, 4), (amount // 2,), 0, 1 << 20) % (room + 1)
    lengths = lengths.at[giver].add(-shifted).at[sink].add(shifted)
    labels = jnp.searchsorted(jnp.cumsum(lengths), jnp.arange(rows * top), side="right").astype(jnp.int32)
    grid = labels.reshape(top, rows).T
    grid = grid[jax.random.permutation(jax.random.fold_in(own, 1), rows)]
    rotation = jax.random.randint(jax.random.fold_in(own, 2), (rows, 1), 0, top)
    return jnp.take_along_axis(grid, (jnp.arange(top)[None, :] + rotation) % top, axis=1)


def portions_of(number_of, total, reach, skew, full):
    portions = [(1 << 20) // math.isqrt(standing ** skew) + 1 for standing in range(1, number_of + 1)]
    largest = reach if full else min(reach, max(-(-total // number_of), total * portions[0] // sum(portions)))
    least = 1 if total - largest >= number_of - 1 else 0
    given, surplus = [largest] + [least] * (number_of - 1), total - largest - least * (number_of - 1)
    while surplus > 0:
        movable = [i for i in range(1, number_of) if given[i] < largest] or [i for i in range(1, number_of) if given[i] < reach]
        mass, budget = sum([portions[i] for i in movable]), surplus
        for i in movable:
            addition = min(reach - given[i], max(1, budget * portions[i] // mass), surplus)
            given[i] = given[i] + addition
            surplus = surplus - addition
    return np.array(given)


def scatter_about(rng, dims, deviation, limit, pieces=(), kind=jnp.bfloat16):
    factor_of = block_scale(rng, dims, pieces, -0.22, 0.18) if pieces else 1.0
    array = jax.random.normal(rng, dims, jnp.float32) * deviation * factor_of
    return jnp.minimum(jnp.maximum(array, -limit), limit).astype(kind)


def setup_inputs(seed: int = 0) -> dict:
    keys = jax.random.split(jax.random.key(seed), 15)
    patches = scatter_about(keys[0], (FRAMES, CLIPS, PATCHES, D), 1.0, 6.0, ((0, 8), (1, 4)))
    temporal_q = draw_temporal_q(jax.random.fold_in(keys[14], 71), 0)
    temporal_k = draw_temporal_k(jax.random.fold_in(keys[14], 71), 0)
    temporal_v = scatter_about(keys[3], (FRAMES, CLIPS, PATCHES, D), 1.0, 6.0, ((0, 8), (1, 4)))
    clip_lengths = plant(jax.random.randint(keys[4], (CLIPS,), 1, FRAMES + 1), jax.random.fold_in(keys[4], 1), 1, FRAMES).astype(jnp.int32)
    w_time = scatter_about(keys[5], (D, D), D ** -0.5, 0.15625)
    gain_space = jnp.clip(1.0 + 0.18 * jax.random.normal(keys[6], (D,), jnp.float32), 0.1, 1.9)
    w_space = draw_w_space(jax.random.fold_in(keys[14], 71), 0)
    w_merge = scatter_about(keys[8], (D, D), D ** -0.5, 0.15625)
    gain_mix = jnp.clip(1.0 + 0.18 * jax.random.normal(keys[9], (D,), jnp.float32), 0.1, 1.9)
    expert_ids_keys = jax.random.split(jax.random.fold_in(keys[10], 1), FRAMES * CLIPS * PATCHES // ROWS_DEV)
    expert_ids_turns = jax.random.permutation(jax.random.fold_in(keys[10], 3), FRAMES * CLIPS * PATCHES // ROWS_DEV)
    expert_ids = jax.vmap(lambda own, number: routed_block(jax.random.fold_in(keys[10], 2), own, number, ROWS_DEV, EXPERTS, 2, CAP, 2))(expert_ids_keys, expert_ids_turns).reshape((FRAMES, CLIPS, PATCHES, 2))
    gate_weights = jnp.clip(0.25 + 0.75 * jax.random.uniform(keys[11], (FRAMES, CLIPS, PATCHES, 2), jnp.float32) ** block_scale(keys[11], (FRAMES, CLIPS, PATCHES, 2), ((0, 8), (1, 4)), -0.2, 0.2), 0.25, 1.0)
    w_expand = scatter_about(keys[12], (DEVICES, D, HID_DEV), D ** -0.5, 0.15625, ((0, 32),))
    w_reduce = scatter_about(keys[13], (DEVICES, HID_DEV, D), FF_EXPERT ** -0.5, 0.078125, ((0, 32),))
    return dict(patches=patches, temporal_q=temporal_q, temporal_k=temporal_k, temporal_v=temporal_v, clip_lengths=clip_lengths, w_time=w_time, gain_space=gain_space, w_space=w_space, w_merge=w_merge, gain_mix=gain_mix, expert_ids=expert_ids, gate_weights=gate_weights, w_expand=w_expand, w_reduce=w_reduce)


epsilon = 1e-06

def layer_norm(values, gain_vector):
    centre = values - lax.optimization_barrier(jnp.mean(values, axis=-1, keepdims=True))
    spread = lax.optimization_barrier(jnp.mean(centre * centre, axis=-1, keepdims=True))
    return (centre * lax.rsqrt(spread + epsilon) * gain_vector.astype(jnp.float32)).astype(jnp.bfloat16)

def softmax_rows(scores):
    top_score = lax.optimization_barrier(jnp.max(scores, axis=-1, keepdims=True))
    powers = jnp.exp(scores - top_score)
    return (powers / lax.optimization_barrier(jnp.sum(powers, axis=-1, keepdims=True))).astype(jnp.bfloat16)

def time_attention(queries, key_rows, value_rows, clip_lengths):
    frame_count, clip_count, place_count, model_width = queries.shape
    head_size = model_width // HEADS

    def split_heads(array_in):
        return array_in.astype(jnp.float32).reshape(frame_count, clip_count, place_count, HEADS, head_size)
    scores = jnp.einsum('fcphd,gcphd->cphfg', split_heads(queries), split_heads(key_rows)) / math.sqrt(head_size)
    valid_keys = jnp.arange(frame_count, dtype=jnp.int32)[None, :] < clip_lengths[:, None]
    scores = jnp.where(valid_keys[:, None, None, None, :], scores, -1e+30)
    weights = softmax_rows(scores)
    attended = jnp.einsum('cphfg,gcphd->fcphd', weights.astype(jnp.float32), split_heads(value_rows))
    return attended.astype(jnp.bfloat16).reshape(frame_count, clip_count, place_count, model_width)

def space_attention(projected):
    clip_count, place_count, triple = projected.shape
    model_width = triple // 3
    head_size = model_width // HEADS
    split_parts = projected.astype(jnp.float32).reshape(clip_count, place_count, 3, HEADS, head_size)
    scores = jnp.einsum('cphd,cqhd->chpq', split_parts[:, :, 0], split_parts[:, :, 1]) / math.sqrt(head_size)
    weights = softmax_rows(scores)
    attended = jnp.einsum('chpq,cqhd->cphd', weights.astype(jnp.float32), split_parts[:, :, 2])
    return attended.astype(jnp.bfloat16).reshape(clip_count, place_count, model_width)

def expert_slots(routes):
    onehot = (routes[..., None] == jnp.arange(EXPERTS, dtype=jnp.int32)).astype(jnp.int32)
    earlier = jnp.cumsum(onehot, axis=-2) - onehot
    return lax.optimization_barrier(jnp.sum(earlier * onehot, axis=-1)).astype(jnp.int32)

def reference(patches, temporal_q, temporal_k, temporal_v, clip_lengths, w_time, gain_space, w_space, w_merge, gain_mix, expert_ids, gate_weights, w_expand, w_reduce):
    model_width = D
    full_shape = patches.shape
    time_mixed = time_attention(temporal_q, temporal_k, temporal_v, clip_lengths)
    after_time = patches.astype(jnp.float32) + jnp.dot(time_mixed.reshape(-1, model_width), w_time, preferred_element_type=jnp.float32).reshape(full_shape)
    normed = layer_norm(after_time, gain_space).reshape(-1, model_width)
    projected = jnp.dot(normed, w_space, preferred_element_type=jnp.float32).astype(jnp.bfloat16)
    projected = projected.reshape(FRAMES, CLIPS, PATCHES, 3 * model_width)
    spatial = lax.map(space_attention, projected)
    after_space = after_time + jnp.dot(spatial.reshape(-1, model_width), w_merge, preferred_element_type=jnp.float32).reshape(full_shape)
    mixed_in = layer_norm(after_space, gain_mix).reshape(DEVICES, ROWS_DEV, model_width)
    routes = expert_ids.reshape(DEVICES, ROWS_DEV * 2).astype(jnp.int32)
    slot_index = expert_slots(routes)
    owner_index = jnp.arange(DEVICES, dtype=jnp.int32)[:, None]
    position = ((routes * DEVICES + owner_index) * CAP + slot_index).reshape(-1).astype(jnp.int32)
    sources = jnp.repeat(mixed_in, 2, axis=1).reshape(-1, model_width)
    buffer_rows = jnp.zeros((EXPERTS * DEVICES * CAP, model_width), jnp.bfloat16).at[position].set(sources)
    expand = w_expand.reshape(EXPERTS, SHARDS, model_width, HID_DEV)
    reduce_part = w_reduce.reshape(EXPERTS, SHARDS, HID_DEV, model_width)

    def run_expert(operands):
        token_rows, expand_blocks, reduce_blocks = operands
        running_sum = jnp.zeros((token_rows.shape[0], model_width), jnp.float32)
        for shard_index in range(SHARDS):
            hidden = jax.nn.gelu(jnp.dot(token_rows, expand_blocks[shard_index], preferred_element_type=jnp.float32), approximate=False).astype(jnp.bfloat16)
            partial_rows = jnp.dot(hidden, reduce_blocks[shard_index], preferred_element_type=jnp.float32).astype(jnp.bfloat16)
            running_sum = running_sum + lax.optimization_barrier(partial_rows).astype(jnp.float32)
        return running_sum
    results = lax.map(run_expert, (buffer_rows.reshape(EXPERTS, DEVICES * CAP, model_width), expand, reduce_part))
    picked = results.reshape(-1, model_width)[position].reshape(DEVICES, ROWS_DEV, 2, model_width)
    gate_rows = gate_weights.reshape(DEVICES, ROWS_DEV, 2, 1)
    expert_mix = picked[:, :, 0] * gate_rows[:, :, 0] + picked[:, :, 1] * gate_rows[:, :, 1]
    return (after_space + expert_mix.reshape(full_shape)).astype(jnp.bfloat16)
```

```python
import functools
import math

import jax
import jax.numpy as jnp
from jax import lax
from jax.experimental import pallas as pl
from jax.experimental.pallas import tpu as pltpu
from jax.sharding import PartitionSpec as P

HEADS = 24
EXPERTS = 32
CAP = 18


epsilon = 1e-06


def layer_norm(values, gain_vector):
    centre = values - jnp.mean(values, axis=-1, keepdims=True)
    spread = jnp.mean(centre * centre, axis=-1, keepdims=True)
    return (centre * lax.rsqrt(spread + epsilon) * gain_vector).astype(jnp.bfloat16)


def softmax_rows(scores):
    top_score = jnp.max(scores, axis=-1, keepdims=True)
    powers = jnp.exp(scores - top_score)
    return (powers / jnp.sum(powers, axis=-1, keepdims=True)).astype(jnp.bfloat16)


def time_kernel(head_size, length_ref, q_ref, k_ref, v_ref, fold_ref, spread_ref, out_ref):
    frame_count, row_count, model_width = k_ref.shape
    lanes = fold_ref.shape[1]
    fold = fold_ref[...]
    spread = spread_ref[...]
    valid = (
        lax.broadcasted_iota(jnp.int32, (frame_count, row_count, lanes), 0) < length_ref[0]
    )

    def one_frame(frame, carry):
        product = q_ref[frame].astype(jnp.float32)[None] * k_ref[...].astype(jnp.float32)
        product = product.reshape(frame_count * row_count, model_width)
        upper = product.astype(jnp.bfloat16)
        lower = (product - upper.astype(jnp.float32)).astype(jnp.bfloat16)
        scores = jnp.dot(upper, fold, preferred_element_type=jnp.float32) + jnp.dot(
            lower, fold, preferred_element_type=jnp.float32
        )
        scores = scores.reshape(frame_count, row_count, lanes) / math.sqrt(head_size)
        scores = jnp.where(valid, scores, -1e30)
        powers = jnp.exp(scores - jnp.max(scores, axis=0, keepdims=True))
        weights = (powers / jnp.sum(powers, axis=0, keepdims=True)).astype(jnp.bfloat16)
        wide = jnp.dot(
            weights.reshape(frame_count * row_count, lanes),
            spread,
            preferred_element_type=jnp.float32,
        ).reshape(frame_count, row_count, model_width)
        out_ref[frame] = jnp.sum(wide * v_ref[...].astype(jnp.float32), axis=0).astype(
            jnp.bfloat16
        )
        return carry

    lax.fori_loop(0, frame_count, one_frame, 0)


def time_attention(queries, key_rows, value_rows, clip_lengths):
    frame_count, place_count, model_width = queries.shape
    head_size = model_width // HEADS
    lanes = -(-HEADS // 128) * 128
    row_block = math.gcd(place_count, 16)
    fold = (
        jnp.arange(model_width, dtype=jnp.int32)[:, None] // head_size
        == jnp.arange(lanes, dtype=jnp.int32)[None, :]
    ).astype(jnp.bfloat16)
    block = pl.BlockSpec((frame_count, row_block, model_width), lambda i: (0, i, 0))
    return pl.pallas_call(
        functools.partial(time_kernel, head_size),
        grid=(place_count // row_block,),
        out_shape=jax.ShapeDtypeStruct(queries.shape, jnp.bfloat16),
        in_specs=[
            pl.BlockSpec(memory_space=pltpu.SMEM),
            block,
            block,
            block,
            pl.BlockSpec((model_width, lanes), lambda i: (0, 0)),
            pl.BlockSpec((lanes, model_width), lambda i: (0, 0)),
        ],
        out_specs=block,
        cost_estimate=pl.CostEstimate(
            flops=6 * frame_count * queries.size * lanes,
            bytes_accessed=8 * queries.size,
            transcendentals=0,
        ),
    )(clip_lengths, queries, key_rows, value_rows, fold, fold.T)


def space_attention(projected):
    clip_count, place_count, triple = projected.shape
    model_width = triple // 3
    head_size = model_width // HEADS
    split_parts = projected.reshape(clip_count, place_count, 3, HEADS, head_size)
    scores = jnp.einsum(
        "cphd,cqhd->chpq",
        split_parts[:, :, 0],
        split_parts[:, :, 1],
        preferred_element_type=jnp.float32,
    ) / math.sqrt(head_size)
    weights = softmax_rows(scores)
    attended = jnp.einsum(
        "chpq,cqhd->cphd", weights, split_parts[:, :, 2], preferred_element_type=jnp.float32
    )
    return attended.astype(jnp.bfloat16).reshape(clip_count, place_count, model_width)


MESH = pl.DeviceIdType.MESH
F32, BF16 = jnp.float32, jnp.bfloat16


def flip(index, mask, size):
    total, weight = 0, 1
    while weight < size:
        here = lax.rem(lax.div(index, jnp.int32(weight)), jnp.int32(2))
        there = lax.rem(lax.div(jnp.int32(mask), jnp.int32(weight)), jnp.int32(2))
        total = total + weight * lax.rem(here + there, jnp.int32(2))
        weight *= 2
    return total


def slot_layout(model_width):
    base = CAP // 16 * 16
    extra = CAP - base
    pieces = base // max(extra, 1)
    while model_width % (pieces * 128):
        pieces -= 1
    return base, extra, pieces, model_width // pieces


def piece_rows(group, base, extra, pieces, piece, turned):
    shape = (group * base, group * extra) if turned else (group * extra, group * base)
    slot = lax.broadcasted_iota(jnp.int32, shape, 1 if turned else 0)
    row = lax.broadcasted_iota(jnp.int32, shape, 0 if turned else 1)
    wanted = lax.div(slot, extra) * base + lax.rem(slot, extra) * pieces + piece
    return (row == wanted).astype(F32).astype(BF16)


def expert_kernel(
    frames,
    clips,
    shards_of,
    sent,
    residual,
    ids_ref,
    gate_ref,
    expand_hbm,
    reduce_hbm,
    out_ref,
    expand,
    reduce,
    arrived,
    result,
    back,
    rows,
    hidden,
    spare,
    spread,
    gates_high,
    gates_low,
    weight_sem,
    send_sem,
    arrive_sem,
    return_sem,
    back_sem,
    own_sem,
):
    model_width = out_ref.shape[1]
    row_count = out_ref.shape[0]
    units = expand.shape[1]
    base, extra, pieces, piece_width = slot_layout(model_width)
    devices = frames * clips
    frame, clip = lax.axis_index("frame"), lax.axis_index("expert")
    me = frame * clips + clip
    order = sorted(range(clips), key=lambda mask: (mask < clips // 2, mask == 0, mask))

    barrier = pltpu.get_barrier_semaphore()

    def partner(place, mask):
        return flip(frame, place, frames), flip(clip, mask, clips)

    for mask in order:

        def greet(place, carry, mask=mask):
            pl.semaphore_signal(
                barrier, inc=1, device_id=partner(place, mask), device_id_type=MESH
            )
            return carry

        lax.fori_loop(0 if mask else 1, frames, greet, 0)

    parts = weight_sem.shape[1]
    loads = []
    for array, (source, target) in enumerate(((expand_hbm, expand), (reduce_hbm, reduce))):
        step = target.shape[0] // parts
        for part in range(parts):
            span = pl.ds(part * step, step)
            loads.append(
                pltpu.make_async_copy(
                    source.at[0, span], target.at[span], weight_sem.at[array, part]
                )
            )
    for load in loads:
        load.start()
    pl.semaphore_wait(barrier, devices - 1)

    def outward(stage, mask, place):
        there = partner(place, mask)
        expert = lax.div(there[0] * clips + there[1], jnp.int32(shards_of))
        return pltpu.make_async_remote_copy(
            src_ref=sent.at[expert],
            dst_ref=arrived.at[stage, place],
            send_sem=send_sem.at[stage, place],
            recv_sem=arrive_sem.at[stage, place],
            device_id=there,
            device_id_type=MESH,
        )

    def homeward(stage, mask, place):
        return pltpu.make_async_remote_copy(
            src_ref=result.at[stage, place],
            dst_ref=back.at[me],
            send_sem=return_sem.at[stage, place],
            recv_sem=back_sem.at[me],
            device_id=partner(place, mask),
            device_id_type=MESH,
        )

    def over(mask, action):
        def step(place, carry):
            action(place)
            return carry

        lax.fori_loop(0 if mask else 1, frames, step, 0)

    for stage, mask in enumerate(order):
        over(mask, lambda place: outward(stage, mask, place).start())
    own_stage = order.index(0)
    own_in = pltpu.make_async_copy(
        sent.at[lax.div(me, jnp.int32(shards_of))], arrived.at[own_stage, 0], own_sem.at[0]
    )
    own_in.start()

    columns = devices * (base + extra)
    lane = lax.broadcasted_iota(jnp.int32, (1, columns), 1)
    tail = lane - devices * base
    owner = jnp.where(tail < 0, lax.div(lane, base), lax.div(tail, extra))
    slot = jnp.where(tail < 0, lax.rem(lane, base), base + lax.rem(tail, extra))
    expert = lax.div(owner, shards_of)
    first = ids_ref[:, 0:1] == expert
    second = ids_ref[:, 1:2] == expert
    named = jnp.where(first | second, 1.0, 0.0)
    below = lax.broadcasted_iota(jnp.int32, (row_count, row_count), 0)
    earlier = (lax.broadcasted_iota(jnp.int32, (row_count, row_count), 1) < below).astype(F32)
    taken = jnp.dot(earlier.astype(BF16), named.astype(BF16), preferred_element_type=F32)
    gates = jnp.where(first, gate_ref[:, 0:1], jnp.where(second, gate_ref[:, 1:2], 0.0))
    gates = jnp.where(taken == slot.astype(F32), gates, 0.0)
    high = gates.astype(BF16)
    gates_high[...] = high
    gates_low[...] = (gates - high.astype(F32)).astype(BF16)

    group = frames * base
    unit_block = math.gcd(units, 512)
    width_block = math.gcd(model_width, 512)
    for stage, mask in sorted(enumerate(order), key=lambda pair: pair[1]):
        over(mask, lambda place: outward(stage, mask, place).wait_recv())
        if mask == 0:
            own_in.wait()
            for load in loads[:parts]:
                load.wait()
        rows[0:group, :] = arrived[stage, :, :, 0:model_width].reshape(group, model_width)
        beside = arrived[stage, :, :, model_width:].reshape(group, piece_width)
        for piece in range(pieces):
            picker = piece_rows(frames, base, extra, pieces, piece, False)
            rows[group:, piece * piece_width : (piece + 1) * piece_width] = jnp.dot(
                picker, beside, preferred_element_type=F32
            ).astype(BF16)

        def widen(block, carry):
            at = pl.ds(pl.multiple_of(block * unit_block, unit_block), unit_block)
            value = jnp.dot(rows[...], expand[:, at], preferred_element_type=F32)
            value = 0.5 * value * (1.0 + lax.erf(value * math.sqrt(0.5)))
            hidden[:, at] = value.astype(BF16)
            return carry

        lax.fori_loop(0, units // unit_block, widen, 0)
        if mask == 0:
            for load in loads[parts:]:
                load.wait()

        def narrow(block, carry):
            at = pl.ds(pl.multiple_of(block * width_block, width_block), width_block)
            value = jnp.dot(hidden[...], reduce[:, at], preferred_element_type=F32).astype(BF16)
            result[stage, :, :, at] = value[0:group].reshape(frames, base, width_block)
            spare[:, at] = value[group:]
            return carry

        lax.fori_loop(0, model_width // width_block, narrow, 0)
        packed = jnp.zeros((group, piece_width), F32)
        for piece in range(pieces):
            packed = packed + jnp.dot(
                piece_rows(frames, base, extra, pieces, piece, True),
                spare[:, piece * piece_width : (piece + 1) * piece_width],
                preferred_element_type=F32,
            )
        result[stage, :, :, model_width:] = packed.astype(BF16).reshape(frames, base, piece_width)
        over(mask, lambda place: homeward(stage, mask, place).start())
        if mask == 0:
            own_out = pltpu.make_async_copy(result.at[stage, 0], back.at[me], own_sem.at[1])
            own_out.start()

    for stage, mask in enumerate(order):

        def settle(place, carry, stage=stage, mask=mask):
            outward(stage, mask, place).wait_send()
            homeward(stage, mask, place).wait_send()
            there = partner(place, mask)
            pltpu.make_async_remote_copy(
                src_ref=result.at[stage, place],
                dst_ref=back.at[there[0] * clips + there[1]],
                send_sem=return_sem.at[stage, place],
                recv_sem=back_sem.at[there[0] * clips + there[1]],
                device_id=there,
                device_id_type=MESH,
            ).wait_recv()
            return carry

        lax.fori_loop(0 if mask else 1, frames, settle, 0)
    own_out.wait()

    beside = back[:, :, model_width:].reshape(devices * base, piece_width)
    for piece in range(pieces):
        picker = piece_rows(devices, base, extra, pieces, piece, False)
        spread[:, piece * piece_width : (piece + 1) * piece_width] = jnp.dot(
            picker, beside, preferred_element_type=F32
        ).astype(BF16)

    def mix(block, carry):
        at = pl.ds(pl.multiple_of(block * width_block, width_block), width_block)
        total = residual[:, at]
        main = back[:, :, at].reshape(devices * base, width_block)
        for gate in (gates_high, gates_low):
            total = total + jnp.dot(
                gate[:, 0 : devices * base], main, preferred_element_type=F32
            )
            total = total + jnp.dot(
                gate[:, devices * base :], spread[:, at], preferred_element_type=F32
            )
        out_ref[:, at] = total.astype(BF16)
        return carry

    lax.fori_loop(0, model_width // width_block, mix, 0)


def expert_mix(sent, residual, ids, gates, w_expand, w_reduce):
    frames, clips = lax.axis_size("frame"), lax.axis_size("expert")
    devices = frames * clips
    row_count, model_width = residual.shape
    units = w_expand.shape[2]
    base, extra, _, piece_width = slot_layout(model_width)
    block = (base, model_width + piece_width)
    group = frames * (base + extra)
    columns = devices * (base + extra)
    parts = 4
    vmem = pl.BlockSpec(memory_space=pltpu.VMEM)
    hbm = pl.BlockSpec(memory_space=pl.ANY)
    dma = pltpu.SemaphoreType.DMA
    return pl.pallas_call(
        functools.partial(expert_kernel, frames, clips, devices // EXPERTS),
        out_shape=jax.ShapeDtypeStruct((row_count, model_width), BF16),
        in_specs=[hbm, vmem, vmem, vmem, hbm, hbm],
        out_specs=vmem,
        scratch_shapes=[
            pltpu.VMEM(w_expand.shape[1:], BF16),
            pltpu.VMEM(w_reduce.shape[1:], BF16),
            pltpu.VMEM((clips, frames) + block, BF16),
            pltpu.VMEM((clips, frames) + block, BF16),
            pltpu.VMEM((devices,) + block, BF16),
            pltpu.VMEM((group, model_width), BF16),
            pltpu.VMEM((group, units), BF16),
            pltpu.VMEM((frames * extra, model_width), BF16),
            pltpu.VMEM((devices * extra, model_width), BF16),
            pltpu.VMEM((row_count, columns), BF16),
            pltpu.VMEM((row_count, columns), BF16),
            dma((2, parts)),
            dma((clips, frames)),
            dma((clips, frames)),
            dma((clips, frames)),
            dma((devices,)),
            dma((2,)),
        ],
        compiler_params=pltpu.CompilerParams(
            collective_id=1, has_side_effects=True, vmem_limit_bytes=60 * 2**20
        ),
        cost_estimate=pl.CostEstimate(
            flops=4 * columns * model_width * units,
            bytes_accessed=4 * model_width * units,
            transcendentals=0,
        ),
    )(sent, residual, ids, gates, w_expand, w_reduce)


def shards(
    patches,
    temporal_q,
    temporal_k,
    temporal_v,
    clip_lengths,
    w_time,
    gain_space,
    w_space,
    w_merge,
    gain_mix,
    expert_ids,
    gate_weights,
    w_expand,
    w_reduce,
):
    local_shape = patches.shape
    model_width = local_shape[-1]
    frame_size = lax.axis_size("frame")

    def by_place(array_in):
        return lax.all_to_all(
            array_in.reshape(frame_size, -1, model_width),
            "frame",
            split_axis=0,
            concat_axis=0,
            tiled=True,
        )

    tube_out = time_attention(
        by_place(temporal_q), by_place(temporal_k), by_place(temporal_v), clip_lengths
    )
    time_mixed = lax.all_to_all(tube_out, "frame", split_axis=0, concat_axis=0, tiled=True)
    after_time = patches.astype(jnp.float32) + jnp.dot(
        time_mixed.reshape(-1, model_width), w_time, preferred_element_type=jnp.float32
    ).reshape(local_shape)
    normed = layer_norm(after_time, gain_space).reshape(-1, model_width)
    projected = jnp.dot(
        normed,
        lax.all_gather(w_space, "frame", axis=1, tiled=True),
        preferred_element_type=jnp.float32,
    ).astype(jnp.bfloat16)
    projected = projected.reshape(local_shape[0], local_shape[1], local_shape[2], 3 * model_width)
    spatial = lax.map(space_attention, projected)
    after_space = after_time + jnp.dot(
        spatial.reshape(-1, model_width), w_merge, preferred_element_type=jnp.float32
    ).reshape(local_shape)
    mixed_in = layer_norm(after_space, gain_mix).reshape(-1, model_width)
    row_count = mixed_in.shape[0]
    ids = expert_ids.reshape(row_count, 2)
    named = jnp.any(ids[:, :, None] == jnp.arange(EXPERTS, dtype=jnp.int32), axis=1)
    earlier = jnp.tri(row_count, k=-1, dtype=jnp.bfloat16)
    taken = jnp.dot(earlier, named.astype(jnp.bfloat16), preferred_element_type=jnp.float32)
    chosen = named[:, :, None] & (
        taken.astype(jnp.int32)[:, :, None] == jnp.arange(CAP, dtype=jnp.int32)
    )
    leaving = jnp.einsum(
        "res,rd->esd", chosen.astype(jnp.bfloat16), mixed_in, preferred_element_type=jnp.float32
    ).astype(jnp.bfloat16)
    base, extra, pieces, piece_width = slot_layout(model_width)
    beside = leaving[:, base:].reshape(EXPERTS, extra * pieces, piece_width)
    beside = jnp.pad(beside, ((0, 0), (0, base - extra * pieces), (0, 0)))
    sent = jnp.concatenate([leaving[:, :base], beside], axis=2)
    return expert_mix(
        sent,
        after_space.reshape(row_count, model_width),
        ids,
        gate_weights.reshape(row_count, 2),
        w_expand,
        w_reduce,
    ).reshape(local_shape)


def solution(mesh):
    return jax.shard_map(
        shards,
        mesh=mesh,
        in_specs=(
            P("frame", "expert", None, None),
            P("frame", "expert", None, None),
            P("frame", "expert", None, None),
            P("frame", "expert", None, None),
            P("expert"),
            P(),
            P(),
            P(None, "frame"),
            P(),
            P(),
            P("frame", "expert", None, None),
            P("frame", "expert", None, None),
            P(("frame", "expert"), None, None),
            P(("frame", "expert"), None, None),
        ),
        out_specs=P("frame", "expert", None, None),
        check_vma=False,
    )
```

```python
import functools
import math

import jax
import jax.numpy as jnp
from jax import lax
from jax.experimental import pallas as pl
from jax.experimental.pallas import tpu as pltpu
from jax.sharding import PartitionSpec as P

HEADS = 24
EXPERTS = 32
CAP = 18


epsilon = 1e-06


def layer_norm(values, gain_vector):
    centre = values - jnp.mean(values, axis=-1, keepdims=True)
    spread = jnp.mean(centre * centre, axis=-1, keepdims=True)
    return (centre * lax.rsqrt(spread + epsilon) * gain_vector).astype(jnp.bfloat16)


MESH = pl.DeviceIdType.MESH
F32, BF16 = jnp.float32, jnp.bfloat16


def flip(index, mask, size):
    total, weight = 0, 1
    while weight < size:
        here = lax.rem(lax.div(index, jnp.int32(weight)), jnp.int32(2))
        there = lax.rem(lax.div(jnp.int32(mask), jnp.int32(weight)), jnp.int32(2))
        total = total + weight * lax.rem(here + there, jnp.int32(2))
        weight *= 2
    return total


def slot_layout(model_width):
    base = CAP // 16 * 16
    extra = CAP - base
    pieces = base // max(extra, 1)
    while model_width % (pieces * 128):
        pieces -= 1
    return base, extra, pieces, model_width // pieces


def piece_rows(group, base, extra, pieces, piece, turned):
    shape = (group * base, group * extra) if turned else (group * extra, group * base)
    slot = lax.broadcasted_iota(jnp.int32, shape, 1 if turned else 0)
    row = lax.broadcasted_iota(jnp.int32, shape, 0 if turned else 1)
    wanted = lax.div(slot, extra) * base + lax.rem(slot, extra) * pieces + piece
    return (row == wanted).astype(F32).astype(BF16)


def shard_layout(depth, columns):
    wide = columns // 128 * 128
    narrow = columns - wide
    return wide, narrow, depth * narrow // wide


def norm_rows(source, gain_ref, target):
    row_count = source.shape[0]
    block = math.gcd(row_count, 64)

    def step(index, carry):
        at = pl.ds(pl.multiple_of(index * block, block), block)
        target[at, :] = layer_norm(source[at, :], gain_ref[...])
        return carry

    lax.fori_loop(0, row_count // block, step, 0)


def attend(query, key_rows, value, head_size, valid):
    lane = lax.broadcasted_iota(jnp.int32, query.shape, 1)
    scaled = query * jnp.asarray(head_size**-0.5, query.dtype)
    mixed = None
    for head in range(query.shape[1] // head_size):
        mine = (lane >= head * head_size) & (lane < (head + 1) * head_size)
        scores = lax.dot_general(
            jnp.where(mine, scaled, jnp.zeros_like(scaled)),
            key_rows,
            (((1,), (1,)), ((), ())),
            preferred_element_type=F32,
        )
        if valid is not None:
            scores = jnp.where(valid, scores, -1e30)
        powers = jnp.exp(scores - jnp.max(scores, axis=-1, keepdims=True))
        share = 1.0 / jnp.sum(powers, axis=-1, keepdims=True)
        found = jnp.dot((powers * share).astype(BF16), value, preferred_element_type=F32)
        mixed = found if mixed is None else jnp.where(mine, found, mixed)
    return mixed.astype(BF16)


def slot_columns(ids_ref, owners, shards_of, base, extra):
    row_count = ids_ref.shape[0]
    lane = lax.broadcasted_iota(jnp.int32, (1, owners * (base + extra)), 1)
    tail = lane - owners * base
    owner = jnp.where(tail < 0, lax.div(lane, base), lax.div(tail, extra))
    slot = jnp.where(tail < 0, lax.rem(lane, base), base + lax.rem(tail, extra))
    expert = lax.div(owner, shards_of)
    first = ids_ref[:, 0:1] == expert
    second = ids_ref[:, 1:2] == expert
    named = jnp.where(first | second, 1.0, 0.0)
    below = lax.broadcasted_iota(jnp.int32, (row_count, row_count), 0)
    earlier = (lax.broadcasted_iota(jnp.int32, (row_count, row_count), 1) < below).astype(F32)
    taken = jnp.dot(earlier.astype(BF16), named.astype(BF16), preferred_element_type=F32)
    here = taken == slot.astype(F32)
    return first & here, second & here


def front_kernel(
    frames,
    clips,
    length_ref,
    query_hbm,
    key_hbm,
    value_hbm,
    patches,
    time_hbm,
    gain_space,
    space_hbm,
    merge_hbm,
    gain_mix,
    ids_ref,
    sent,
    residual,
    queries,
    key_rows,
    values,
    tubes,
    mixed,
    w_time,
    w_merge,
    local,
    shard,
    columns,
    projected,
    stream,
    rows,
    chosen,
    beside,
    load_sem,
    own_sem,
    part_send,
    part_come,
    home_send,
    home_come,
    flat_send,
    flat_come,
    deep_send,
    deep_come,
    pair_send,
    pair_come,
    whole_sem,
):
    row_count, model_width = residual.shape
    head_size = model_width // HEADS
    blocks, _, block_rows, _ = queries.shape
    places = blocks * block_rows
    base, extra, pieces, piece_width = slot_layout(model_width)
    shard_width = local.shape[1]
    wide, narrow, fold = shard_layout(model_width, shard_width)
    frame, clip = lax.axis_index("frame"), lax.axis_index("expert")
    half = lax.rem(clip, 2)

    def beside_frame(mask):
        return flip(frame, mask, frames), clip

    partner = (frame, clip + 1 - 2 * half)
    barrier = pltpu.get_barrier_semaphore()

    def greet(mask, carry):
        pl.semaphore_signal(barrier, inc=1, device_id=beside_frame(mask), device_id_type=MESH)
        return carry

    lax.fori_loop(1, frames, greet, 0)
    pl.semaphore_signal(barrier, inc=1, device_id=partner, device_id_type=MESH)

    load_local = pltpu.make_async_copy(space_hbm, local, load_sem.at[0])
    load_time = pltpu.make_async_copy(time_hbm, w_time, load_sem.at[1])
    load_merge = pltpu.make_async_copy(merge_hbm, w_merge, load_sem.at[2])
    load_local.start()
    pl.semaphore_wait(barrier, frames)

    def remote(source, target, send_sem, come_sem, there):
        return pltpu.make_async_remote_copy(
            src_ref=source,
            dst_ref=target,
            send_sem=send_sem,
            recv_sem=come_sem,
            device_id=there,
            device_id_type=MESH,
        )

    quarters = 4
    evens = range(2, frames, 2)
    place_of = {mask: number for number, mask in enumerate(evens)}

    def way(mask, quarter):
        low = mask & -mask
        return low if quarter % 2 == 0 else 1 << (mask.bit_length() - 1)

    def span(quarter, which):
        depth = (model_width if quarter < 2 else fold) // 4
        start = (0 if quarter < 2 else model_width) + quarter % 2 * depth
        start = start + which * (2 * depth)
        return pl.ds(pl.multiple_of(start, 16), depth)

    def flat(mask, quarter, early=False):
        by = way(mask, quarter)
        at = span(quarter, half)
        source = space_hbm.at[at, 0:wide] if early else shard.at[mask ^ by, at]
        sems = (place_of[mask], quarter)
        return remote(
            source, shard.at[mask, at], flat_send.at[sems], flat_come.at[sems], beside_frame(by)
        )

    def deep(mask, quarter, which):
        piece = shard.at[mask, span(quarter, which)]
        sems = (place_of[mask], quarter)
        return remote(piece, piece, deep_send.at[sems], deep_come.at[sems], partner)

    def pair(mask, quarter, which, number):
        at = span(quarter, which)
        sems = (place_of[mask], number, quarter)
        return remote(
            shard.at[mask, at],
            shard.at[mask + 1, at],
            pair_send.at[sems],
            pair_come.at[sems],
            beside_frame(1),
        )

    single = [mask for mask in evens if mask & (mask - 1) == 0]
    double = [mask for mask in evens if mask & (mask - 1)]
    double.sort(key=lambda mask: (bin(mask).count("1"), mask))
    opening = [(mask, 1 if number == 0 else 0) for number, mask in enumerate(single)]
    closing = [
        (mask, quarter)
        for mask in single
        for quarter in range(quarters)
        if (mask, quarter) not in opening
    ]
    for mask, quarter in opening:
        flat(mask, quarter, True).start()

    arrays = ((query_hbm, queries), (key_hbm, key_rows), (value_hbm, values))

    def part(array, block, mask):
        there = flip(frame, mask, frames)
        source, target = arrays[array]
        start = pl.multiple_of(there * places + block * block_rows, block_rows)
        return source.at[pl.ds(start, block_rows)], target.at[block], there

    def part_out(array, block, mask):
        source, target, there = part(array, block, mask)
        return remote(
            source,
            target.at[frame],
            part_send.at[array, block, mask],
            part_come.at[array, block, mask],
            (there, clip),
        )

    def part_in(array, block, mask):
        source, target, there = part(array, block, mask)
        return remote(
            source,
            target.at[there],
            part_send.at[array, block, mask],
            part_come.at[array, block, mask],
            (there, clip),
        )

    def own_part(array, block):
        source, target, _ = part(array, block, 0)
        return pltpu.make_async_copy(source, target.at[frame], own_sem.at[array, block])

    def each(action):
        def step(mask, carry):
            action(mask)
            return carry

        lax.fori_loop(1, frames, step, 0)

    def send_parts(block):
        for array in range(3):
            each(lambda mask: part_out(array, block, mask).start())
            own_part(array, block).start()

    def home(block, mask, incoming):
        there = flip(frame, mask, frames)
        start = pl.multiple_of(
            (there if incoming else frame) * places + block * block_rows, block_rows
        )
        return remote(
            tubes.at[block, there],
            mixed.at[pl.ds(start, block_rows)],
            home_send.at[block, mask],
            home_come.at[block, mask],
            (there, clip),
        )

    group = frames * block_rows
    row = lax.broadcasted_iota(jnp.int32, (group, group), 0)
    column = lax.broadcasted_iota(jnp.int32, (group, group), 1)
    valid = (lax.rem(row, block_rows) == lax.rem(column, block_rows)) & (
        lax.div(column, block_rows) < length_ref[0]
    )

    def time_block(block):
        for array in range(3):
            each(lambda mask: part_in(array, block, mask).wait_recv())
            own_part(array, block).wait()

        def heads(index, carry):
            at = pl.ds(pl.multiple_of(index * 128, 128), 128)
            found = attend(
                queries[block, :, :, at].reshape(group, 128),
                key_rows[block, :, :, at].reshape(group, 128),
                values[block, :, :, at].reshape(group, 128),
                head_size,
                valid,
            )
            tubes[block, :, :, at] = found.reshape(frames, block_rows, 128)
            return carry

        lax.fori_loop(0, model_width // 128, heads, 0)
        each(lambda mask: home(block, mask, False).start())
        start = pl.multiple_of(frame * places + block * block_rows, block_rows)
        mixed[pl.ds(start, block_rows), :] = tubes[block, frame]

    def pass_on(mask, quarter):
        flat(mask, quarter).wait_recv()
        for later in double:
            if later ^ way(later, quarter) == mask:
                flat(later, quarter).start()
        deep(mask, quarter, half).start()
        pair(mask, quarter, half, 0).start()

    send_parts(0)
    load_local.wait()
    shard[0, 0:model_width, :] = local[:, 0:wide]
    lanes = 128 // narrow
    deepness = fold * (wide // 128)
    for tile in range(wide // 128):
        folded = jnp.zeros((fold, 128), F32)
        for turn in range(lanes):
            start = turn * deepness + tile * fold
            source = lax.broadcasted_iota(jnp.int32, (narrow, 128), 0)
            target = lax.broadcasted_iota(jnp.int32, (narrow, 128), 1)
            shift = (target == source + turn * narrow).astype(F32).astype(BF16)
            folded = folded + jnp.dot(
                local[start : start + fold, wide:], shift, preferred_element_type=F32
            )
        shard[0, model_width:, tile * 128 : (tile + 1) * 128] = folded.astype(BF16)
    own_shard = remote(
        shard.at[0], shard.at[1], whole_sem.at[0], whole_sem.at[1], beside_frame(1)
    )
    own_shard.start()
    load_time.start()
    load_merge.start()

    for mask, quarter in opening:
        pass_on(mask, quarter)
    for mask, quarter in closing:
        flat(mask, quarter).start()
    for block in range(1, blocks):
        send_parts(block)

    first, second = slot_columns(ids_ref, EXPERTS, 1, base, extra)
    hits = jnp.where(first | second, 1.0, 0.0)
    chosen[...] = hits[:, 0 : EXPERTS * base].T.astype(BF16)
    beside[...] = hits[:, EXPERTS * base :].T.astype(BF16)

    time_block(0)
    ready, rest = list(opening), list(closing)
    for mask in double:
        for quarter in range(quarters):
            from_ready = (mask ^ way(mask, quarter), quarter) in ready
            (ready if from_ready else rest).append((mask, quarter))
    arrivals = ready + rest
    for mask, quarter in arrivals[len(opening) :]:
        pass_on(mask, quarter)
    for block in range(1, blocks):
        time_block(block)
    for mask, quarter in arrivals:
        deep(mask, quarter, 1 - half).wait_recv()
        pair(mask, quarter, 1 - half, 1).start()

    for block in range(blocks):
        each(lambda mask: home(block, mask, True).wait_recv())
    load_time.wait()
    width_block = math.gcd(model_width, 512)

    def time_columns(index, carry):
        at = pl.ds(pl.multiple_of(index * width_block, width_block), width_block)
        stream[:, at] = patches[:, at].astype(F32) + jnp.dot(
            mixed[...], w_time[:, at], preferred_element_type=F32
        )
        return carry

    lax.fori_loop(0, model_width // width_block, time_columns, 0)
    norm_rows(stream, gain_space, rows)

    own_shard.wait_recv()
    for mask, quarter in arrivals:
        pair(mask, quarter, half, 0).wait_recv()
        pair(mask, quarter, 1 - half, 1).wait_recv()

    def project(mask, carry):
        columns[mask, :, 0:wide] = jnp.dot(
            rows[...], shard[mask, 0:model_width, :], preferred_element_type=F32
        ).astype(BF16)
        folded = jnp.concatenate(
            [
                shard[mask, model_width:, tile * 128 : (tile + 1) * 128]
                for tile in range(wide // 128)
            ],
            axis=0,
        )
        for turn in range(lanes):
            found = jnp.dot(
                rows[:, turn * deepness : (turn + 1) * deepness],
                folded,
                preferred_element_type=F32,
            )[:, turn * narrow : (turn + 1) * narrow]
            total = found if turn == 0 else total + found
        columns[mask, :, wide:] = total.astype(BF16)
        return carry

    lax.fori_loop(0, frames, project, 0)
    for number in range(frames):
        projected[:, number * shard_width : (number + 1) * shard_width] = columns[
            flip(frame, number, frames)
        ]

    def space_heads(index, carry):
        def at(which):
            return pl.ds(pl.multiple_of(which * model_width + index * 128, 128), 128)

        mixed[:, at(0)] = attend(
            projected[:, at(0)], projected[:, at(1)], projected[:, at(2)], head_size, None
        )
        return carry

    lax.fori_loop(0, model_width // 128, space_heads, 0)
    load_merge.wait()

    def merge_columns(index, carry):
        at = pl.ds(pl.multiple_of(index * width_block, width_block), width_block)
        residual[:, at] = stream[:, at] + jnp.dot(
            mixed[...], w_merge[:, at], preferred_element_type=F32
        )
        return carry

    lax.fori_loop(0, model_width // width_block, merge_columns, 0)
    norm_rows(residual, gain_mix, rows)

    def leave(index, carry):
        at = pl.ds(pl.multiple_of(index * width_block, width_block), width_block)
        found = jnp.dot(chosen[...], rows[:, at], preferred_element_type=F32).astype(BF16)
        sent[:, :, at] = found.reshape(EXPERTS, base, width_block)
        return carry

    lax.fori_loop(0, model_width // width_block, leave, 0)
    packed = jnp.zeros((EXPERTS * base, piece_width), F32)
    for piece in range(pieces):
        found = jnp.dot(
            beside[...],
            rows[:, piece * piece_width : (piece + 1) * piece_width],
            preferred_element_type=F32,
        ).astype(BF16)
        packed = packed + jnp.dot(
            piece_rows(EXPERTS, base, extra, pieces, piece, True), found, preferred_element_type=F32
        )
    sent[:, :, model_width:] = packed.astype(BF16).reshape(EXPERTS, base, piece_width)

    for block in range(blocks):
        for array in range(3):
            each(lambda mask: part_out(array, block, mask).wait_send())
        each(lambda mask: home(block, mask, False).wait_send())
    own_shard.wait_send()
    for mask, quarter in arrivals:
        flat(mask, quarter, (mask, quarter) in opening).wait_send()
        deep(mask, quarter, half).wait_send()
        pair(mask, quarter, half, 0).wait_send()
        pair(mask, quarter, 1 - half, 1).wait_send()


def front(
    clip_lengths,
    temporal_q,
    temporal_k,
    temporal_v,
    patches,
    w_time,
    gain_space,
    w_space,
    w_merge,
    gain_mix,
    ids,
):
    frames, clips = lax.axis_size("frame"), lax.axis_size("expert")
    row_count, model_width = patches.shape
    places = row_count // frames
    block_rows = math.gcd(places, 16)
    blocks = places // block_rows
    shard_width = w_space.shape[1]
    wide, _, fold = shard_layout(model_width, shard_width)
    base, extra, _, piece_width = slot_layout(model_width)
    vmem = pl.BlockSpec(memory_space=pltpu.VMEM)
    hbm = pl.BlockSpec(memory_space=pl.ANY)
    dma = pltpu.SemaphoreType.DMA
    tube = pltpu.VMEM((blocks, frames, block_rows, model_width), BF16)
    square = pltpu.VMEM((model_width, model_width), BF16)
    others = frames // 2 - 1
    quarters = 4
    return pl.pallas_call(
        functools.partial(front_kernel, frames, clips),
        out_shape=(
            jax.ShapeDtypeStruct((EXPERTS, base, model_width + piece_width), BF16),
            jax.ShapeDtypeStruct((row_count, model_width), F32),
        ),
        in_specs=[
            pl.BlockSpec(memory_space=pltpu.SMEM),
            hbm,
            hbm,
            hbm,
            vmem,
            hbm,
            vmem,
            hbm,
            hbm,
            vmem,
            vmem,
        ],
        out_specs=(vmem, vmem),
        scratch_shapes=[
            tube,
            tube,
            tube,
            tube,
            pltpu.VMEM((row_count, model_width), BF16),
            square,
            square,
            pltpu.VMEM((model_width, shard_width), BF16),
            pltpu.VMEM((frames, model_width + fold, wide), BF16),
            pltpu.VMEM((frames, row_count, shard_width), BF16),
            pltpu.VMEM((row_count, 3 * model_width), BF16),
            pltpu.VMEM((row_count, model_width), F32),
            pltpu.VMEM((row_count, model_width), BF16),
            pltpu.VMEM((EXPERTS * base, row_count), BF16),
            pltpu.VMEM((EXPERTS * extra, row_count), BF16),
            dma((3,)),
            dma((3, blocks)),
            dma((3, blocks, frames)),
            dma((3, blocks, frames)),
            dma((blocks, frames)),
            dma((blocks, frames)),
            dma((others, quarters)),
            dma((others, quarters)),
            dma((others, quarters)),
            dma((others, quarters)),
            dma((others, 2, quarters)),
            dma((others, 2, quarters)),
            dma((2,)),
        ],
        compiler_params=pltpu.CompilerParams(
            collective_id=0, has_side_effects=True, vmem_limit_bytes=60 * 2**20
        ),
        cost_estimate=pl.CostEstimate(
            flops=10 * row_count * model_width * model_width,
            bytes_accessed=10 * model_width * model_width,
            transcendentals=0,
        ),
    )(
        clip_lengths,
        temporal_q,
        temporal_k,
        temporal_v,
        patches,
        w_time,
        gain_space,
        w_space,
        w_merge,
        gain_mix,
        ids,
    )


def expert_kernel(
    frames,
    clips,
    shards_of,
    sent,
    residual,
    ids_ref,
    gate_ref,
    expand_hbm,
    reduce_hbm,
    out_ref,
    expand,
    reduce,
    arrived,
    result,
    back,
    rows,
    hidden,
    spare,
    spread,
    gates_high,
    gates_low,
    weight_sem,
    send_sem,
    arrive_sem,
    return_sem,
    back_sem,
    own_sem,
):
    model_width = out_ref.shape[1]
    row_count = out_ref.shape[0]
    units = expand.shape[1]
    base, extra, pieces, piece_width = slot_layout(model_width)
    devices = frames * clips
    frame, clip = lax.axis_index("frame"), lax.axis_index("expert")
    me = frame * clips + clip
    order = sorted(range(clips), key=lambda mask: (mask < clips // 2, mask == 0, mask))

    barrier = pltpu.get_barrier_semaphore()

    def partner(place, mask):
        return flip(frame, place, frames), flip(clip, mask, clips)

    for mask in order:

        def greet(place, carry, mask=mask):
            pl.semaphore_signal(
                barrier, inc=1, device_id=partner(place, mask), device_id_type=MESH
            )
            return carry

        lax.fori_loop(0 if mask else 1, frames, greet, 0)

    parts = weight_sem.shape[1]
    loads = []
    for array, (source, target) in enumerate(((expand_hbm, expand), (reduce_hbm, reduce))):
        step = target.shape[0] // parts
        for part in range(parts):
            span = pl.ds(part * step, step)
            loads.append(
                pltpu.make_async_copy(
                    source.at[0, span], target.at[span], weight_sem.at[array, part]
                )
            )
    for load in loads:
        load.start()
    pl.semaphore_wait(barrier, devices - 1)

    def outward(stage, mask, place):
        there = partner(place, mask)
        expert = lax.div(there[0] * clips + there[1], jnp.int32(shards_of))
        return pltpu.make_async_remote_copy(
            src_ref=sent.at[expert],
            dst_ref=arrived.at[stage, place],
            send_sem=send_sem.at[stage, place],
            recv_sem=arrive_sem.at[stage, place],
            device_id=there,
            device_id_type=MESH,
        )

    def homeward(stage, mask, place):
        return pltpu.make_async_remote_copy(
            src_ref=result.at[stage, place],
            dst_ref=back.at[me],
            send_sem=return_sem.at[stage, place],
            recv_sem=back_sem.at[me],
            device_id=partner(place, mask),
            device_id_type=MESH,
        )

    def over(mask, action):
        def step(place, carry):
            action(place)
            return carry

        lax.fori_loop(0 if mask else 1, frames, step, 0)

    for stage, mask in enumerate(order):
        over(mask, lambda place: outward(stage, mask, place).start())
    own_stage = order.index(0)
    own_in = pltpu.make_async_copy(
        sent.at[lax.div(me, jnp.int32(shards_of))], arrived.at[own_stage, 0], own_sem.at[0]
    )
    own_in.start()

    first, second = slot_columns(ids_ref, devices, shards_of, base, extra)
    gates = jnp.where(first, gate_ref[:, 0:1], jnp.where(second, gate_ref[:, 1:2], 0.0))
    high = gates.astype(BF16)
    gates_high[...] = high
    gates_low[...] = (gates - high.astype(F32)).astype(BF16)

    group = frames * base
    unit_block = math.gcd(units, 512)
    width_block = math.gcd(model_width, 512)
    for stage, mask in sorted(enumerate(order), key=lambda pair: pair[1]):
        over(mask, lambda place: outward(stage, mask, place).wait_recv())
        if mask == 0:
            own_in.wait()
            for load in loads[:parts]:
                load.wait()
        rows[0:group, :] = arrived[stage, :, :, 0:model_width].reshape(group, model_width)
        beside = arrived[stage, :, :, model_width:].reshape(group, piece_width)
        for piece in range(pieces):
            picker = piece_rows(frames, base, extra, pieces, piece, False)
            rows[group:, piece * piece_width : (piece + 1) * piece_width] = jnp.dot(
                picker, beside, preferred_element_type=F32
            ).astype(BF16)

        def widen(block, carry):
            at = pl.ds(pl.multiple_of(block * unit_block, unit_block), unit_block)
            value = jnp.dot(rows[...], expand[:, at], preferred_element_type=F32)
            value = 0.5 * value * (1.0 + lax.erf(value * math.sqrt(0.5)))
            hidden[:, at] = value.astype(BF16)
            return carry

        lax.fori_loop(0, units // unit_block, widen, 0)
        if mask == 0:
            for load in loads[parts:]:
                load.wait()

        def narrow(block, carry):
            at = pl.ds(pl.multiple_of(block * width_block, width_block), width_block)
            value = jnp.dot(hidden[...], reduce[:, at], preferred_element_type=F32).astype(BF16)
            result[stage, :, :, at] = value[0:group].reshape(frames, base, width_block)
            spare[:, at] = value[group:]
            return carry

        lax.fori_loop(0, model_width // width_block, narrow, 0)
        packed = jnp.zeros((group, piece_width), F32)
        for piece in range(pieces):
            packed = packed + jnp.dot(
                piece_rows(frames, base, extra, pieces, piece, True),
                spare[:, piece * piece_width : (piece + 1) * piece_width],
                preferred_element_type=F32,
            )
        result[stage, :, :, model_width:] = packed.astype(BF16).reshape(frames, base, piece_width)
        over(mask, lambda place: homeward(stage, mask, place).start())
        if mask == 0:
            own_out = pltpu.make_async_copy(result.at[stage, 0], back.at[me], own_sem.at[1])
            own_out.start()

    for stage, mask in enumerate(order):

        def settle(place, carry, stage=stage, mask=mask):
            outward(stage, mask, place).wait_send()
            homeward(stage, mask, place).wait_send()
            there = partner(place, mask)
            pltpu.make_async_remote_copy(
                src_ref=result.at[stage, place],
                dst_ref=back.at[there[0] * clips + there[1]],
                send_sem=return_sem.at[stage, place],
                recv_sem=back_sem.at[there[0] * clips + there[1]],
                device_id=there,
                device_id_type=MESH,
            ).wait_recv()
            return carry

        lax.fori_loop(0 if mask else 1, frames, settle, 0)
    own_out.wait()

    beside = back[:, :, model_width:].reshape(devices * base, piece_width)
    for piece in range(pieces):
        picker = piece_rows(devices, base, extra, pieces, piece, False)
        spread[:, piece * piece_width : (piece + 1) * piece_width] = jnp.dot(
            picker, beside, preferred_element_type=F32
        ).astype(BF16)

    def mix(block, carry):
        at = pl.ds(pl.multiple_of(block * width_block, width_block), width_block)
        total = residual[:, at]
        main = back[:, :, at].reshape(devices * base, width_block)
        for gate in (gates_high, gates_low):
            total = total + jnp.dot(
                gate[:, 0 : devices * base], main, preferred_element_type=F32
            )
            total = total + jnp.dot(
                gate[:, devices * base :], spread[:, at], preferred_element_type=F32
            )
        out_ref[:, at] = total.astype(BF16)
        return carry

    lax.fori_loop(0, model_width // width_block, mix, 0)


def expert_mix(sent, residual, ids, gates, w_expand, w_reduce):
    frames, clips = lax.axis_size("frame"), lax.axis_size("expert")
    devices = frames * clips
    row_count, model_width = residual.shape
    units = w_expand.shape[2]
    base, extra, _, piece_width = slot_layout(model_width)
    block = (base, model_width + piece_width)
    group = frames * (base + extra)
    columns = devices * (base + extra)
    parts = 4
    vmem = pl.BlockSpec(memory_space=pltpu.VMEM)
    hbm = pl.BlockSpec(memory_space=pl.ANY)
    dma = pltpu.SemaphoreType.DMA
    return pl.pallas_call(
        functools.partial(expert_kernel, frames, clips, devices // EXPERTS),
        out_shape=jax.ShapeDtypeStruct((row_count, model_width), BF16),
        in_specs=[hbm, vmem, vmem, vmem, hbm, hbm],
        out_specs=vmem,
        scratch_shapes=[
            pltpu.VMEM(w_expand.shape[1:], BF16),
            pltpu.VMEM(w_reduce.shape[1:], BF16),
            pltpu.VMEM((clips, frames) + block, BF16),
            pltpu.VMEM((clips, frames) + block, BF16),
            pltpu.VMEM((devices,) + block, BF16),
            pltpu.VMEM((group, model_width), BF16),
            pltpu.VMEM((group, units), BF16),
            pltpu.VMEM((frames * extra, model_width), BF16),
            pltpu.VMEM((devices * extra, model_width), BF16),
            pltpu.VMEM((row_count, columns), BF16),
            pltpu.VMEM((row_count, columns), BF16),
            dma((2, parts)),
            dma((clips, frames)),
            dma((clips, frames)),
            dma((clips, frames)),
            dma((devices,)),
            dma((2,)),
        ],
        compiler_params=pltpu.CompilerParams(
            collective_id=1, has_side_effects=True, vmem_limit_bytes=60 * 2**20
        ),
        cost_estimate=pl.CostEstimate(
            flops=4 * columns * model_width * units,
            bytes_accessed=4 * model_width * units,
            transcendentals=0,
        ),
    )(sent, residual, ids, gates, w_expand, w_reduce)


def shards(
    patches,
    temporal_q,
    temporal_k,
    temporal_v,
    clip_lengths,
    w_time,
    gain_space,
    w_space,
    w_merge,
    gain_mix,
    expert_ids,
    gate_weights,
    w_expand,
    w_reduce,
):
    local_shape = patches.shape
    model_width = local_shape[-1]
    flat = (-1, model_width)
    ids = expert_ids.reshape(-1, 2)
    sent, residual = front(
        clip_lengths,
        temporal_q.reshape(flat),
        temporal_k.reshape(flat),
        temporal_v.reshape(flat),
        patches.reshape(flat),
        w_time,
        gain_space.reshape(1, model_width),
        w_space,
        w_merge,
        gain_mix.reshape(1, model_width),
        ids,
    )
    mixed = expert_mix(sent, residual, ids, gate_weights.reshape(-1, 2), w_expand, w_reduce)
    return mixed.reshape(local_shape)


def solution(mesh):
    return jax.shard_map(
        shards,
        mesh=mesh,
        in_specs=(
            P("frame", "expert", None, None),
            P("frame", "expert", None, None),
            P("frame", "expert", None, None),
            P("frame", "expert", None, None),
            P("expert"),
            P(),
            P(),
            P(None, "frame"),
            P(),
            P(),
            P("frame", "expert", None, None),
            P("frame", "expert", None, None),
            P(("frame", "expert"), None, None),
            P(("frame", "expert"), None, None),
        ),
        out_specs=P("frame", "expert", None, None),
        check_vma=False,
    )
```

```python
import functools
import math

import jax
import jax.numpy as jnp
from jax import lax
from jax.experimental import pallas as pl
from jax.experimental.pallas import tpu as pltpu
from jax.sharding import PartitionSpec as P

HEADS = 24
EXPERTS = 32
CAP = 18


epsilon = 1e-06


def layer_norm(values, gain_vector):
    centre = values - jnp.mean(values, axis=-1, keepdims=True)
    spread = jnp.mean(centre * centre, axis=-1, keepdims=True)
    return (centre * lax.rsqrt(spread + epsilon) * gain_vector).astype(jnp.bfloat16)


MESH = pl.DeviceIdType.MESH
F32, BF16 = jnp.float32, jnp.bfloat16


def flip(index, mask, size):
    total, weight = 0, 1
    while weight < size:
        here = lax.rem(lax.div(index, jnp.int32(weight)), jnp.int32(2))
        there = lax.rem(lax.div(jnp.int32(mask), jnp.int32(weight)), jnp.int32(2))
        total = total + weight * lax.rem(here + there, jnp.int32(2))
        weight *= 2
    return total


def slot_layout(model_width):
    base = CAP // 16 * 16
    extra = CAP - base
    pieces = base // max(extra, 1)
    while model_width % (pieces * 128):
        pieces -= 1
    return base, extra, pieces, model_width // pieces


def piece_rows(group, base, extra, pieces, piece, turned):
    shape = (group * base, group * extra) if turned else (group * extra, group * base)
    slot = lax.broadcasted_iota(jnp.int32, shape, 1 if turned else 0)
    row = lax.broadcasted_iota(jnp.int32, shape, 0 if turned else 1)
    wanted = lax.div(slot, extra) * base + lax.rem(slot, extra) * pieces + piece
    return (row == wanted).astype(F32).astype(BF16)


def norm_rows(source, gain_ref, target):
    row_count = source.shape[0]
    block = math.gcd(row_count, 64)

    def step(index, carry):
        at = pl.ds(pl.multiple_of(index * block, block), block)
        target[at, :] = layer_norm(source[at, :], gain_ref[...].reshape(1, -1))
        return carry

    lax.fori_loop(0, row_count // block, step, 0)


def attend(query, key_rows, value, head_size, valid):
    lane = lax.broadcasted_iota(jnp.int32, query.shape, 1)
    scaled = query * jnp.asarray(head_size**-0.5, query.dtype)
    mixed = None
    for head in range(query.shape[1] // head_size):
        mine = (lane >= head * head_size) & (lane < (head + 1) * head_size)
        scores = lax.dot_general(
            jnp.where(mine, scaled, jnp.zeros_like(scaled)),
            key_rows,
            (((1,), (1,)), ((), ())),
            preferred_element_type=F32,
        )
        if valid is not None:
            scores = jnp.where(valid, scores, -1e30)
        powers = jnp.exp(scores - jnp.max(scores, axis=-1, keepdims=True))
        share = 1.0 / jnp.sum(powers, axis=-1, keepdims=True)
        found = jnp.dot((powers * share).astype(BF16), value, preferred_element_type=F32)
        mixed = found if mixed is None else jnp.where(mine, found, mixed)
    return mixed.astype(BF16)


def slot_rows(ids_ref, owners, shards_of, base, extra):
    row_count = ids_ref.shape[1]
    place = lax.broadcasted_iota(jnp.int32, (owners * (base + extra), 1), 0)
    tail = place - owners * base
    owner = jnp.where(tail < 0, lax.div(place, base), lax.div(tail, extra))
    slot = jnp.where(tail < 0, lax.rem(place, base), base + lax.rem(tail, extra))
    expert = lax.div(owner, shards_of)
    first = ids_ref[0:1, :] == expert
    second = ids_ref[1:2, :] == expert
    named = jnp.where(first | second, 1.0, 0.0)
    above = lax.broadcasted_iota(jnp.int32, (row_count, row_count), 1)
    earlier = (lax.broadcasted_iota(jnp.int32, (row_count, row_count), 0) < above).astype(F32)
    taken = jnp.dot(named.astype(BF16), earlier.astype(BF16), preferred_element_type=F32)
    here = taken == slot.astype(F32)
    return first & here, second & here


def front_kernel(
    frames,
    clips,
    length_ref,
    query_hbm,
    key_hbm,
    value_hbm,
    patches,
    time_hbm,
    gain_space,
    space_hbm,
    merge_hbm,
    gain_mix,
    ids_ref,
    sent,
    residual,
    queries,
    key_rows,
    values,
    tubes,
    mixed,
    w_time,
    w_merge,
    shards_in,
    projected,
    stream,
    rows,
    chosen,
    beside,
    load_sem,
    own_sem,
    part_send,
    part_come,
    home_send,
    home_come,
    flat_send,
    flat_come,
    deep_send,
    deep_come,
    pair_send,
    pair_come,
    whole_sem,
):
    row_count, model_width = residual.shape
    head_size = model_width // HEADS
    blocks, _, block_rows, _ = queries.shape
    places = blocks * block_rows
    base, extra, pieces, piece_width = slot_layout(model_width)
    shard_width = space_hbm.shape[0]
    frame, clip = lax.axis_index("frame"), lax.axis_index("expert")
    half = lax.rem(clip, 2)

    def beside_frame(mask):
        return flip(frame, mask, frames), clip

    partner = (frame, clip + 1 - 2 * half)
    barrier = pltpu.get_barrier_semaphore()

    def greet(mask, carry):
        pl.semaphore_signal(barrier, inc=1, device_id=beside_frame(mask), device_id_type=MESH)
        return carry

    lax.fori_loop(1, frames, greet, 0)
    pl.semaphore_signal(barrier, inc=1, device_id=partner, device_id_type=MESH)

    own_rows = pl.ds(pl.multiple_of(frame * shard_width, 16), shard_width)
    load_own = pltpu.make_async_copy(space_hbm, shards_in.at[own_rows], load_sem.at[0])
    load_time = pltpu.make_async_copy(time_hbm, w_time, load_sem.at[1])
    load_merge = pltpu.make_async_copy(merge_hbm, w_merge, load_sem.at[2])
    pl.semaphore_wait(barrier, frames)

    def remote(source, target, send_sem, come_sem, there):
        return pltpu.make_async_remote_copy(
            src_ref=source,
            dst_ref=target,
            send_sem=send_sem,
            recv_sem=come_sem,
            device_id=there,
            device_id_type=MESH,
        )

    quarters = 2
    evens = range(2, frames, 2)
    place_of = {mask: number for number, mask in enumerate(evens)}

    def way(mask, quarter):
        return mask & -mask if quarter == 0 else 1 << (mask.bit_length() - 1)

    def span(start, quarter, which):
        share = shard_width // 2
        first = -(-share // 32) * 16
        start = start + which * share + (0, first)[quarter]
        return pl.ds(pl.multiple_of(start, 16), (first, share - first)[quarter])

    def shard_of(mask):
        return flip(frame, mask, frames) * shard_width

    def flat(mask, quarter):
        by = way(mask, quarter)
        target = shards_in.at[span(shard_of(mask ^ by), quarter, half)]
        source = target
        if mask == by:
            source = space_hbm.at[span(0, quarter, half)]
        sems = (place_of[mask], quarter)
        return remote(source, target, flat_send.at[sems], flat_come.at[sems], beside_frame(by))

    def deep(mask, quarter, which):
        piece = shards_in.at[span(shard_of(mask), quarter, which)]
        sems = (place_of[mask], quarter)
        return remote(piece, piece, deep_send.at[sems], deep_come.at[sems], partner)

    def pair(mask, quarter, which, number):
        piece = shards_in.at[span(shard_of(mask), quarter, which)]
        sems = (place_of[mask], number, quarter)
        return remote(piece, piece, pair_send.at[sems], pair_come.at[sems], beside_frame(1))

    single = [mask for mask in evens if mask & (mask - 1) == 0]
    double = [mask for mask in evens if mask & (mask - 1)]
    double.sort(key=lambda mask: (bin(mask).count("1"), mask))
    opening = [(mask, 1 if number == 0 else 0) for number, mask in enumerate(single)]
    closing = [
        (mask, quarter)
        for mask in single
        for quarter in range(quarters)
        if (mask, quarter) not in opening
    ]
    for mask, quarter in opening:
        flat(mask, quarter).start()

    arrays = ((query_hbm, queries), (key_hbm, key_rows), (value_hbm, values))

    def part(array, block, mask):
        there = flip(frame, mask, frames)
        source, target = arrays[array]
        start = pl.multiple_of(there * places + block * block_rows, block_rows)
        return source.at[pl.ds(start, block_rows)], target.at[block], there

    def part_out(array, block, mask):
        source, target, there = part(array, block, mask)
        return remote(
            source,
            target.at[frame],
            part_send.at[array, block, mask],
            part_come.at[array, block, mask],
            (there, clip),
        )

    def part_in(array, block, mask):
        source, target, there = part(array, block, mask)
        return remote(
            source,
            target.at[there],
            part_send.at[array, block, mask],
            part_come.at[array, block, mask],
            (there, clip),
        )

    def own_part(array, block):
        source, target, _ = part(array, block, 0)
        return pltpu.make_async_copy(source, target.at[frame], own_sem.at[array, block])

    def each(action):
        def step(mask, carry):
            action(mask)
            return carry

        lax.fori_loop(1, frames, step, 0)

    def send_parts(block):
        for array in range(3):
            each(lambda mask: part_out(array, block, mask).start())
            own_part(array, block).start()

    def home(block, mask, incoming):
        there = flip(frame, mask, frames)
        start = pl.multiple_of(
            (there if incoming else frame) * places + block * block_rows, block_rows
        )
        return remote(
            tubes.at[block, there],
            mixed.at[pl.ds(start, block_rows)],
            home_send.at[block, mask],
            home_come.at[block, mask],
            (there, clip),
        )

    group = frames * block_rows
    row = lax.broadcasted_iota(jnp.int32, (group, group), 0)
    column = lax.broadcasted_iota(jnp.int32, (group, group), 1)
    valid = (lax.rem(row, block_rows) == lax.rem(column, block_rows)) & (
        lax.div(column, block_rows) < length_ref[0]
    )

    def time_block(block):
        for array in range(3):
            each(lambda mask: part_in(array, block, mask).wait_recv())
            own_part(array, block).wait()

        def heads(index, carry):
            at = pl.ds(pl.multiple_of(index * 128, 128), 128)
            found = attend(
                queries[block, :, :, at].reshape(group, 128),
                key_rows[block, :, :, at].reshape(group, 128),
                values[block, :, :, at].reshape(group, 128),
                head_size,
                valid,
            )
            tubes[block, :, :, at] = found.reshape(frames, block_rows, 128)
            return carry

        lax.fori_loop(0, model_width // 128, heads, 0, unroll=4)
        each(lambda mask: home(block, mask, False).start())
        start = pl.multiple_of(frame * places + block * block_rows, block_rows)
        mixed[pl.ds(start, block_rows), :] = tubes[block, frame]

    def pass_on(mask, quarter):
        flat(mask, quarter).wait_recv()
        for later in double:
            if later ^ way(later, quarter) == mask:
                flat(later, quarter).start()
        deep(mask, quarter, half).start()
        pair(mask, quarter, half, 0).start()

    send_parts(0)
    own_shard = remote(
        space_hbm, shards_in.at[own_rows], whole_sem.at[0], whole_sem.at[1], beside_frame(1)
    )
    own_shard.start()
    load_own.start()
    load_time.start()
    load_merge.start()

    for mask, quarter in opening:
        pass_on(mask, quarter)
    for mask, quarter in closing:
        flat(mask, quarter).start()
    for block in range(1, blocks):
        send_parts(block)

    first, second = slot_rows(ids_ref, EXPERTS, 1, base, extra)
    hits = jnp.where(first | second, 1.0, 0.0).astype(BF16)
    chosen[...] = hits[0 : EXPERTS * base]
    beside[...] = hits[EXPERTS * base :]

    time_block(0)
    ready, rest = list(opening), list(closing)
    for mask in double:
        for quarter in range(quarters):
            from_ready = (mask ^ way(mask, quarter), quarter) in ready
            (ready if from_ready else rest).append((mask, quarter))
    arrivals = ready + rest
    for mask, quarter in arrivals[len(opening) :]:
        pass_on(mask, quarter)
    for block in range(1, blocks):
        time_block(block)
    for mask, quarter in arrivals:
        deep(mask, quarter, 1 - half).wait_recv()
        pair(mask, quarter, 1 - half, 1).start()

    for block in range(blocks):
        each(lambda mask: home(block, mask, True).wait_recv())
    load_time.wait()
    width_block = math.gcd(model_width, 512)

    def time_columns(index, carry):
        at = pl.ds(pl.multiple_of(index * width_block, width_block), width_block)
        stream[:, at] = patches[:, at].astype(F32) + jnp.dot(
            mixed[...], w_time[:, at], preferred_element_type=F32
        )
        return carry

    lax.fori_loop(0, model_width // width_block, time_columns, 0)
    norm_rows(stream, gain_space, rows)

    load_own.wait()
    own_shard.wait_recv()
    for mask, quarter in arrivals:
        pair(mask, quarter, half, 0).wait_recv()
        pair(mask, quarter, 1 - half, 1).wait_recv()

    project_block = math.gcd(3 * model_width, 512)

    def project(index, carry):
        at = pl.ds(pl.multiple_of(index * project_block, project_block), project_block)
        projected[:, at] = lax.dot_general(
            rows[...], shards_in[at, :], (((1,), (1,)), ((), ())), preferred_element_type=F32
        ).astype(BF16)
        return carry

    lax.fori_loop(0, 3 * model_width // project_block, project, 0)

    def space_heads(index, carry):
        def at(which):
            return pl.ds(pl.multiple_of(which * model_width + index * 128, 128), 128)

        mixed[:, at(0)] = attend(
            projected[:, at(0)], projected[:, at(1)], projected[:, at(2)], head_size, None
        )
        return carry

    lax.fori_loop(0, model_width // 128, space_heads, 0, unroll=4)
    load_merge.wait()

    def merge_columns(index, carry):
        at = pl.ds(pl.multiple_of(index * width_block, width_block), width_block)
        residual[:, at] = stream[:, at] + jnp.dot(
            mixed[...], w_merge[:, at], preferred_element_type=F32
        )
        return carry

    lax.fori_loop(0, model_width // width_block, merge_columns, 0)
    norm_rows(residual, gain_mix, rows)

    def leave(index, carry):
        at = pl.ds(pl.multiple_of(index * width_block, width_block), width_block)
        found = jnp.dot(chosen[...], rows[:, at], preferred_element_type=F32).astype(BF16)
        sent[:, :, at] = found.reshape(EXPERTS, base, width_block)
        return carry

    lax.fori_loop(0, model_width // width_block, leave, 0)
    packed = jnp.zeros((EXPERTS * base, piece_width), F32)
    for piece in range(pieces):
        found = jnp.dot(
            beside[...],
            rows[:, piece * piece_width : (piece + 1) * piece_width],
            preferred_element_type=F32,
        ).astype(BF16)
        packed = packed + jnp.dot(
            piece_rows(EXPERTS, base, extra, pieces, piece, True), found, preferred_element_type=F32
        )
    sent[:, :, model_width:] = packed.astype(BF16).reshape(EXPERTS, base, piece_width)

    for block in range(blocks):
        for array in range(3):
            each(lambda mask: part_out(array, block, mask).wait_send())
        each(lambda mask: home(block, mask, False).wait_send())
    own_shard.wait_send()
    for mask, quarter in arrivals:
        flat(mask, quarter).wait_send()
        deep(mask, quarter, half).wait_send()
        pair(mask, quarter, half, 0).wait_send()
        pair(mask, quarter, 1 - half, 1).wait_send()


def front(
    clip_lengths,
    temporal_q,
    temporal_k,
    temporal_v,
    patches,
    w_time,
    gain_space,
    w_space,
    w_merge,
    gain_mix,
    ids,
):
    frames, clips = lax.axis_size("frame"), lax.axis_size("expert")
    row_count, model_width = patches.shape
    places = row_count // frames
    block_rows = math.gcd(places, 16)
    blocks = places // block_rows
    shard_width = w_space.shape[0]
    base, extra, _, piece_width = slot_layout(model_width)
    vmem = pl.BlockSpec(memory_space=pltpu.VMEM)
    hbm = pl.BlockSpec(memory_space=pl.ANY)
    dma = pltpu.SemaphoreType.DMA
    tube = pltpu.VMEM((blocks, frames, block_rows, model_width), BF16)
    square = pltpu.VMEM((model_width, model_width), BF16)
    others = frames // 2 - 1
    quarters = 2
    return pl.pallas_call(
        functools.partial(front_kernel, frames, clips),
        out_shape=(
            jax.ShapeDtypeStruct((EXPERTS, base, model_width + piece_width), BF16),
            jax.ShapeDtypeStruct((row_count, model_width), F32),
        ),
        in_specs=[
            pl.BlockSpec(memory_space=pltpu.SMEM),
            hbm,
            hbm,
            hbm,
            vmem,
            hbm,
            vmem,
            hbm,
            hbm,
            vmem,
            vmem,
        ],
        out_specs=(vmem, vmem),
        scratch_shapes=[
            tube,
            tube,
            tube,
            tube,
            pltpu.VMEM((row_count, model_width), BF16),
            square,
            square,
            pltpu.VMEM((frames * shard_width, model_width), BF16),
            pltpu.VMEM((row_count, 3 * model_width), BF16),
            pltpu.VMEM((row_count, model_width), F32),
            pltpu.VMEM((row_count, model_width), BF16),
            pltpu.VMEM((EXPERTS * base, row_count), BF16),
            pltpu.VMEM((EXPERTS * extra, row_count), BF16),
            dma((3,)),
            dma((3, blocks)),
            dma((3, blocks, frames)),
            dma((3, blocks, frames)),
            dma((blocks, frames)),
            dma((blocks, frames)),
            dma((others, quarters)),
            dma((others, quarters)),
            dma((others, quarters)),
            dma((others, quarters)),
            dma((others, 2, quarters)),
            dma((others, 2, quarters)),
            dma((2,)),
        ],
        compiler_params=pltpu.CompilerParams(
            collective_id=0, has_side_effects=True, vmem_limit_bytes=60 * 2**20
        ),
        cost_estimate=pl.CostEstimate(
            flops=10 * row_count * model_width * model_width,
            bytes_accessed=10 * model_width * model_width,
            transcendentals=0,
        ),
    )(
        clip_lengths,
        temporal_q,
        temporal_k,
        temporal_v,
        patches,
        w_time,
        gain_space,
        w_space,
        w_merge,
        gain_mix,
        ids,
    )


def expert_kernel(
    frames,
    clips,
    shards_of,
    sent,
    residual,
    ids_ref,
    gate_ref,
    expand_hbm,
    reduce_hbm,
    out_ref,
    expand,
    reduce,
    arrived,
    result,
    back,
    rows,
    hidden,
    spare,
    spread,
    gates_high,
    gates_low,
    weight_sem,
    send_sem,
    arrive_sem,
    return_sem,
    back_sem,
    own_sem,
):
    model_width = out_ref.shape[1]
    row_count = out_ref.shape[0]
    units = expand.shape[1]
    base, extra, pieces, piece_width = slot_layout(model_width)
    devices = frames * clips
    frame, clip = lax.axis_index("frame"), lax.axis_index("expert")
    me = frame * clips + clip
    order = sorted(range(clips), key=lambda mask: (mask < clips // 2, mask == 0, mask))

    barrier = pltpu.get_barrier_semaphore()

    def partner(place, mask):
        return flip(frame, place, frames), flip(clip, mask, clips)

    for mask in order:

        def greet(place, carry, mask=mask):
            pl.semaphore_signal(
                barrier, inc=1, device_id=partner(place, mask), device_id_type=MESH
            )
            return carry

        lax.fori_loop(0 if mask else 1, frames, greet, 0)

    parts = weight_sem.shape[1]
    loads = []
    for array, (source, target) in enumerate(((expand_hbm, expand), (reduce_hbm, reduce))):
        step = target.shape[0] // parts
        for part in range(parts):
            span = pl.ds(part * step, step)
            loads.append(
                pltpu.make_async_copy(
                    source.at[0, span], target.at[span], weight_sem.at[array, part]
                )
            )
    for load in loads:
        load.start()
    pl.semaphore_wait(barrier, devices - 1)

    def outward(stage, mask, place):
        there = partner(place, mask)
        expert = lax.div(there[0] * clips + there[1], jnp.int32(shards_of))
        return pltpu.make_async_remote_copy(
            src_ref=sent.at[expert],
            dst_ref=arrived.at[stage, place],
            send_sem=send_sem.at[stage, place],
            recv_sem=arrive_sem.at[stage, place],
            device_id=there,
            device_id_type=MESH,
        )

    def homeward(stage, mask, place):
        return pltpu.make_async_remote_copy(
            src_ref=result.at[stage, place],
            dst_ref=back.at[me],
            send_sem=return_sem.at[stage, place],
            recv_sem=back_sem.at[me],
            device_id=partner(place, mask),
            device_id_type=MESH,
        )

    def over(mask, action):
        def step(place, carry):
            action(place)
            return carry

        lax.fori_loop(0 if mask else 1, frames, step, 0)

    for stage, mask in enumerate(order):
        over(mask, lambda place: outward(stage, mask, place).start())
    own_stage = order.index(0)
    own_in = pltpu.make_async_copy(
        sent.at[lax.div(me, jnp.int32(shards_of))], arrived.at[own_stage, 0], own_sem.at[0]
    )
    own_in.start()

    first, second = slot_rows(ids_ref, devices, shards_of, base, extra)
    gates = jnp.where(first, gate_ref[0:1, :], jnp.where(second, gate_ref[1:2, :], 0.0))
    for at in (slice(0, devices * base), slice(devices * base, devices * (base + extra))):
        turned = gates[at].T
        high = turned.astype(BF16)
        gates_high[:, at] = high
        gates_low[:, at] = (turned - high.astype(F32)).astype(BF16)

    group = frames * base
    unit_block = math.gcd(units, 512)
    width_block = math.gcd(model_width, 512)
    for stage, mask in sorted(enumerate(order), key=lambda pair: pair[1]):
        over(mask, lambda place: outward(stage, mask, place).wait_recv())
        if mask == 0:
            own_in.wait()
            for load in loads[:parts]:
                load.wait()
        rows[0:group, :] = arrived[stage, :, :, 0:model_width].reshape(group, model_width)
        beside = arrived[stage, :, :, model_width:].reshape(group, piece_width)
        for piece in range(pieces):
            picker = piece_rows(frames, base, extra, pieces, piece, False)
            rows[group:, piece * piece_width : (piece + 1) * piece_width] = jnp.dot(
                picker, beside, preferred_element_type=F32
            ).astype(BF16)

        def widen(block, carry):
            at = pl.ds(pl.multiple_of(block * unit_block, unit_block), unit_block)
            value = jnp.dot(rows[...], expand[:, at], preferred_element_type=F32)
            value = 0.5 * value * (1.0 + lax.erf(value * math.sqrt(0.5)))
            hidden[:, at] = value.astype(BF16)
            return carry

        lax.fori_loop(0, units // unit_block, widen, 0)
        if mask == 0:
            for load in loads[parts:]:
                load.wait()

        def narrow(block, carry):
            at = pl.ds(pl.multiple_of(block * width_block, width_block), width_block)
            value = jnp.dot(hidden[...], reduce[:, at], preferred_element_type=F32).astype(BF16)
            result[stage, :, :, at] = value[0:group].reshape(frames, base, width_block)
            spare[:, at] = value[group:]
            return carry

        lax.fori_loop(0, model_width // width_block, narrow, 0)
        packed = jnp.zeros((group, piece_width), F32)
        for piece in range(pieces):
            packed = packed + jnp.dot(
                piece_rows(frames, base, extra, pieces, piece, True),
                spare[:, piece * piece_width : (piece + 1) * piece_width],
                preferred_element_type=F32,
            )
        result[stage, :, :, model_width:] = packed.astype(BF16).reshape(frames, base, piece_width)
        over(mask, lambda place: homeward(stage, mask, place).start())
        if mask == 0:
            own_out = pltpu.make_async_copy(result.at[stage, 0], back.at[me], own_sem.at[1])
            own_out.start()

    for stage, mask in enumerate(order):

        def settle(place, carry, stage=stage, mask=mask):
            outward(stage, mask, place).wait_send()
            homeward(stage, mask, place).wait_send()
            there = partner(place, mask)
            pltpu.make_async_remote_copy(
                src_ref=result.at[stage, place],
                dst_ref=back.at[there[0] * clips + there[1]],
                send_sem=return_sem.at[stage, place],
                recv_sem=back_sem.at[there[0] * clips + there[1]],
                device_id=there,
                device_id_type=MESH,
            ).wait_recv()
            return carry

        lax.fori_loop(0 if mask else 1, frames, settle, 0)
    own_out.wait()

    beside = back[:, :, model_width:].reshape(devices * base, piece_width)
    for piece in range(pieces):
        picker = piece_rows(devices, base, extra, pieces, piece, False)
        spread[:, piece * piece_width : (piece + 1) * piece_width] = jnp.dot(
            picker, beside, preferred_element_type=F32
        ).astype(BF16)

    def mix(block, carry):
        at = pl.ds(pl.multiple_of(block * width_block, width_block), width_block)
        total = residual[:, at]
        main = back[:, :, at].reshape(devices * base, width_block)
        for gate in (gates_high, gates_low):
            total = total + jnp.dot(
                gate[:, 0 : devices * base], main, preferred_element_type=F32
            )
            total = total + jnp.dot(
                gate[:, devices * base :], spread[:, at], preferred_element_type=F32
            )
        out_ref[:, at] = total.astype(BF16)
        return carry

    lax.fori_loop(0, model_width // width_block, mix, 0)


def expert_mix(sent, residual, ids, gates, w_expand, w_reduce):
    frames, clips = lax.axis_size("frame"), lax.axis_size("expert")
    devices = frames * clips
    row_count, model_width = residual.shape
    units = w_expand.shape[2]
    base, extra, _, piece_width = slot_layout(model_width)
    block = (base, model_width + piece_width)
    group = frames * (base + extra)
    columns = devices * (base + extra)
    parts = 4
    vmem = pl.BlockSpec(memory_space=pltpu.VMEM)
    hbm = pl.BlockSpec(memory_space=pl.ANY)
    dma = pltpu.SemaphoreType.DMA
    return pl.pallas_call(
        functools.partial(expert_kernel, frames, clips, devices // EXPERTS),
        out_shape=jax.ShapeDtypeStruct((row_count, model_width), BF16),
        in_specs=[hbm, vmem, vmem, vmem, hbm, hbm],
        out_specs=vmem,
        scratch_shapes=[
            pltpu.VMEM(w_expand.shape[1:], BF16),
            pltpu.VMEM(w_reduce.shape[1:], BF16),
            pltpu.VMEM((clips, frames) + block, BF16),
            pltpu.VMEM((clips, frames) + block, BF16),
            pltpu.VMEM((devices,) + block, BF16),
            pltpu.VMEM((group, model_width), BF16),
            pltpu.VMEM((group, units), BF16),
            pltpu.VMEM((frames * extra, model_width), BF16),
            pltpu.VMEM((devices * extra, model_width), BF16),
            pltpu.VMEM((row_count, columns), BF16),
            pltpu.VMEM((row_count, columns), BF16),
            dma((2, parts)),
            dma((clips, frames)),
            dma((clips, frames)),
            dma((clips, frames)),
            dma((devices,)),
            dma((2,)),
        ],
        compiler_params=pltpu.CompilerParams(
            collective_id=1, has_side_effects=True, vmem_limit_bytes=60 * 2**20
        ),
        cost_estimate=pl.CostEstimate(
            flops=4 * columns * model_width * units,
            bytes_accessed=4 * model_width * units,
            transcendentals=0,
        ),
    )(sent, residual, ids, gates, w_expand, w_reduce)


def shards(
    patches,
    temporal_q,
    temporal_k,
    temporal_v,
    clip_lengths,
    w_time,
    gain_space,
    w_space,
    w_merge,
    gain_mix,
    expert_ids,
    gate_weights,
    w_expand,
    w_reduce,
):
    local_shape = patches.shape
    model_width = local_shape[-1]
    flat = (-1, model_width)
    ids = expert_ids.reshape(-1, 2).T
    sent, residual = front(
        clip_lengths,
        temporal_q.reshape(flat),
        temporal_k.reshape(flat),
        temporal_v.reshape(flat),
        patches.reshape(flat),
        w_time,
        gain_space,
        w_space.T,
        w_merge,
        gain_mix,
        ids,
    )
    mixed = expert_mix(sent, residual, ids, gate_weights.reshape(-1, 2).T, w_expand, w_reduce)
    return mixed.reshape(local_shape)


def solution(mesh):
    return jax.shard_map(
        shards,
        mesh=mesh,
        in_specs=(
            P("frame", "expert", None, None),
            P("frame", "expert", None, None),
            P("frame", "expert", None, None),
            P("frame", "expert", None, None),
            P("expert"),
            P(),
            P(),
            P(None, "frame"),
            P(),
            P(),
            P("frame", "expert", None, None),
            P("frame", "expert", None, None),
            P(("frame", "expert"), None, None),
            P(("frame", "expert"), None, None),
        ),
        out_specs=P("frame", "expert", None, None),
        check_vma=False,
    )
```

```python
import functools
import math

import jax
import jax.numpy as jnp
from jax import lax
from jax.experimental import pallas as pl
from jax.experimental.pallas import tpu as pltpu
from jax.sharding import PartitionSpec as P

HEADS = 24
EXPERTS = 32
CAP = 18


epsilon = 1e-06


def layer_norm(values, gain_vector):
    centre = values - jnp.mean(values, axis=-1, keepdims=True)
    spread = jnp.mean(centre * centre, axis=-1, keepdims=True)
    return (centre * lax.rsqrt(spread + epsilon) * gain_vector).astype(jnp.bfloat16)


MESH = pl.DeviceIdType.MESH
F32, BF16 = jnp.float32, jnp.bfloat16


def flip(index, mask, size):
    total, weight = 0, 1
    while weight < size:
        here = lax.rem(lax.div(index, jnp.int32(weight)), jnp.int32(2))
        there = lax.rem(lax.div(jnp.int32(mask), jnp.int32(weight)), jnp.int32(2))
        total = total + weight * lax.rem(here + there, jnp.int32(2))
        weight *= 2
    return total


def slot_layout(model_width):
    base = CAP // 16 * 16
    extra = CAP - base
    pieces = base // max(extra, 1)
    while model_width % (pieces * 128):
        pieces -= 1
    return base, extra, pieces, model_width // pieces


def piece_rows(group, base, extra, pieces, piece, turned):
    shape = (group * base, group * extra) if turned else (group * extra, group * base)
    slot = lax.broadcasted_iota(jnp.int32, shape, 1 if turned else 0)
    row = lax.broadcasted_iota(jnp.int32, shape, 0 if turned else 1)
    wanted = lax.div(slot, extra) * base + lax.rem(slot, extra) * pieces + piece
    return (row == wanted).astype(F32).astype(BF16)


def norm_rows(source, gain_ref, target):
    row_count = source.shape[0]
    block = math.gcd(row_count, 64)

    def step(index, carry):
        at = pl.ds(pl.multiple_of(index * block, block), block)
        target[at, :] = layer_norm(source[at, :], gain_ref[...].reshape(1, -1))
        return carry

    lax.fori_loop(0, row_count // block, step, 0)


def attend(query, key_rows, value, head_size, valid):
    lane = lax.broadcasted_iota(jnp.int32, query.shape, 1)
    scaled = query * jnp.asarray(head_size**-0.5, query.dtype)
    mixed = None
    for head in range(query.shape[1] // head_size):
        mine = (lane >= head * head_size) & (lane < (head + 1) * head_size)
        scores = lax.dot_general(
            jnp.where(mine, scaled, jnp.zeros_like(scaled)),
            key_rows,
            (((1,), (1,)), ((), ())),
            preferred_element_type=F32,
        )
        if valid is not None:
            scores = jnp.where(valid, scores, -1e30)
        powers = jnp.exp(scores - jnp.max(scores, axis=-1, keepdims=True))
        found = jnp.dot(powers.astype(BF16), value, preferred_element_type=F32)
        found = found * (1.0 / jnp.sum(powers, axis=-1, keepdims=True))
        mixed = found if mixed is None else jnp.where(mine, found, mixed)
    return mixed.astype(BF16)


def slot_rows(ids_ref, owners, shards_of, base, extra):
    row_count = ids_ref.shape[1]
    place = lax.broadcasted_iota(jnp.int32, (owners * (base + extra), 1), 0)
    tail = place - owners * base
    owner = jnp.where(tail < 0, lax.div(place, base), lax.div(tail, extra))
    slot = jnp.where(tail < 0, lax.rem(place, base), base + lax.rem(tail, extra))
    expert = lax.div(owner, shards_of)
    first = ids_ref[0:1, :] == expert
    second = ids_ref[1:2, :] == expert
    named = jnp.where(first | second, 1.0, 0.0)
    above = lax.broadcasted_iota(jnp.int32, (row_count, row_count), 1)
    earlier = (lax.broadcasted_iota(jnp.int32, (row_count, row_count), 0) < above).astype(F32)
    taken = jnp.dot(named.astype(BF16), earlier.astype(BF16), preferred_element_type=F32)
    here = taken == slot.astype(F32)
    return first & here, second & here


def front_kernel(
    frames,
    clips,
    length_ref,
    query_hbm,
    key_hbm,
    value_hbm,
    patches,
    time_hbm,
    gain_space,
    space_hbm,
    merge_hbm,
    gain_mix,
    ids_ref,
    sent,
    residual,
    queries,
    key_rows,
    values,
    tubes,
    mixed,
    w_time,
    w_merge,
    shards_in,
    projected,
    stream,
    rows,
    chosen,
    beside,
    load_sem,
    own_sem,
    part_send,
    part_come,
    home_send,
    home_come,
    flat_send,
    flat_come,
    deep_send,
    deep_come,
    pair_send,
    pair_come,
    whole_sem,
):
    row_count, model_width = residual.shape
    head_size = model_width // HEADS
    blocks, _, block_rows, _ = queries.shape
    places = blocks * block_rows
    base, extra, pieces, piece_width = slot_layout(model_width)
    shard_width = space_hbm.shape[0]
    frame, clip = lax.axis_index("frame"), lax.axis_index("expert")
    half = lax.rem(clip, 2)

    def beside_frame(mask):
        return flip(frame, mask, frames), clip

    partner = (frame, clip + 1 - 2 * half)
    barrier = pltpu.get_barrier_semaphore()

    def greet(mask, carry):
        pl.semaphore_signal(barrier, inc=1, device_id=beside_frame(mask), device_id_type=MESH)
        return carry

    lax.fori_loop(1, frames, greet, 0)
    pl.semaphore_signal(barrier, inc=1, device_id=partner, device_id_type=MESH)

    own_rows = pl.ds(pl.multiple_of(frame * shard_width, 16), shard_width)
    load_own = pltpu.make_async_copy(space_hbm, shards_in.at[own_rows], load_sem.at[0])
    load_time = pltpu.make_async_copy(time_hbm, w_time, load_sem.at[1])
    load_merge = pltpu.make_async_copy(merge_hbm, w_merge, load_sem.at[2])
    pl.semaphore_wait(barrier, frames)

    def remote(source, target, send_sem, come_sem, there):
        return pltpu.make_async_remote_copy(
            src_ref=source,
            dst_ref=target,
            send_sem=send_sem,
            recv_sem=come_sem,
            device_id=there,
            device_id_type=MESH,
        )

    quarters = 2
    evens = range(2, frames, 2)
    place_of = {mask: number for number, mask in enumerate(evens)}

    def way(mask, quarter):
        return mask & -mask if quarter == 0 else 1 << (mask.bit_length() - 1)

    def span(start, quarter, which):
        share = shard_width // 2
        first = -(-share // 32) * 16
        start = start + which * share + (0, first)[quarter]
        return pl.ds(pl.multiple_of(start, 16), (first, share - first)[quarter])

    def shard_of(mask):
        return flip(frame, mask, frames) * shard_width

    def flat(mask, quarter):
        by = way(mask, quarter)
        target = shards_in.at[span(shard_of(mask ^ by), quarter, half)]
        source = target
        if mask == by:
            source = space_hbm.at[span(0, quarter, half)]
        sems = (place_of[mask], quarter)
        return remote(source, target, flat_send.at[sems], flat_come.at[sems], beside_frame(by))

    def deep(mask, quarter, which):
        piece = shards_in.at[span(shard_of(mask), quarter, which)]
        sems = (place_of[mask], quarter)
        return remote(piece, piece, deep_send.at[sems], deep_come.at[sems], partner)

    def pair(mask, quarter, which, number):
        piece = shards_in.at[span(shard_of(mask), quarter, which)]
        sems = (place_of[mask], number, quarter)
        return remote(piece, piece, pair_send.at[sems], pair_come.at[sems], beside_frame(1))

    single = [mask for mask in evens if mask & (mask - 1) == 0]
    double = [mask for mask in evens if mask & (mask - 1)]
    double.sort(key=lambda mask: (bin(mask).count("1"), mask))
    opening = [(mask, 1 if number == 0 else 0) for number, mask in enumerate(single)]
    closing = [
        (mask, quarter)
        for mask in single
        for quarter in range(quarters)
        if (mask, quarter) not in opening
    ]
    for mask, quarter in opening:
        flat(mask, quarter).start()

    arrays = ((query_hbm, queries), (key_hbm, key_rows), (value_hbm, values))

    def part(array, block, mask):
        there = flip(frame, mask, frames)
        source, target = arrays[array]
        start = pl.multiple_of(there * places + block * block_rows, block_rows)
        return source.at[pl.ds(start, block_rows)], target.at[block], there

    def part_out(array, block, mask):
        source, target, there = part(array, block, mask)
        return remote(
            source,
            target.at[frame],
            part_send.at[array, block, mask],
            part_come.at[array, block, mask],
            (there, clip),
        )

    def part_in(array, block, mask):
        source, target, there = part(array, block, mask)
        return remote(
            source,
            target.at[there],
            part_send.at[array, block, mask],
            part_come.at[array, block, mask],
            (there, clip),
        )

    def own_part(array, block):
        source, target, _ = part(array, block, 0)
        return pltpu.make_async_copy(source, target.at[frame], own_sem.at[array, block])

    def each(action):
        def step(mask, carry):
            action(mask)
            return carry

        lax.fori_loop(1, frames, step, 0)

    def send_parts(block):
        for array in range(3):
            each(lambda mask: part_out(array, block, mask).start())
            own_part(array, block).start()

    def home(block, mask, incoming):
        there = flip(frame, mask, frames)
        start = pl.multiple_of(
            (there if incoming else frame) * places + block * block_rows, block_rows
        )
        return remote(
            tubes.at[block, there],
            mixed.at[pl.ds(start, block_rows)],
            home_send.at[block, mask],
            home_come.at[block, mask],
            (there, clip),
        )

    group = frames * block_rows
    row = lax.broadcasted_iota(jnp.int32, (group, group), 0)
    column = lax.broadcasted_iota(jnp.int32, (group, group), 1)
    valid = (lax.rem(row, block_rows) == lax.rem(column, block_rows)) & (
        lax.div(column, block_rows) < length_ref[0]
    )

    def time_block(block):
        for array in range(3):
            each(lambda mask: part_in(array, block, mask).wait_recv())
            own_part(array, block).wait()

        def heads(index, carry):
            at = pl.ds(pl.multiple_of(index * 128, 128), 128)
            found = attend(
                queries[block, :, :, at].reshape(group, 128),
                key_rows[block, :, :, at].reshape(group, 128),
                values[block, :, :, at].reshape(group, 128),
                head_size,
                valid,
            )
            tubes[block, :, :, at] = found.reshape(frames, block_rows, 128)
            return carry

        lax.fori_loop(0, model_width // 128, heads, 0, unroll=6)
        each(lambda mask: home(block, mask, False).start())
        start = pl.multiple_of(frame * places + block * block_rows, block_rows)
        mixed[pl.ds(start, block_rows), :] = tubes[block, frame]

    def pass_on(mask, quarter):
        flat(mask, quarter).wait_recv()
        for later in double:
            if later ^ way(later, quarter) == mask:
                flat(later, quarter).start()
        deep(mask, quarter, half).start()
        pair(mask, quarter, half, 0).start()

    send_parts(0)
    own_shard = remote(
        space_hbm, shards_in.at[own_rows], whole_sem.at[0], whole_sem.at[1], beside_frame(1)
    )
    own_shard.start()
    load_own.start()
    load_time.start()
    load_merge.start()

    for mask, quarter in opening:
        pass_on(mask, quarter)
    for mask, quarter in closing:
        flat(mask, quarter).start()
    for block in range(1, blocks):
        send_parts(block)

    first, second = slot_rows(ids_ref, EXPERTS, 1, base, extra)
    hits = jnp.where(first | second, 1.0, 0.0).astype(BF16)
    chosen[...] = hits[0 : EXPERTS * base]
    beside[...] = hits[EXPERTS * base :]

    time_block(0)
    ready, rest = list(opening), list(closing)
    for mask in double:
        for quarter in range(quarters):
            from_ready = (mask ^ way(mask, quarter), quarter) in ready
            (ready if from_ready else rest).append((mask, quarter))
    arrivals = ready + rest
    for mask, quarter in arrivals[len(opening) :]:
        pass_on(mask, quarter)
    for block in range(1, blocks):
        time_block(block)
    for mask, quarter in arrivals:
        deep(mask, quarter, 1 - half).wait_recv()
        pair(mask, quarter, 1 - half, 1).start()

    for block in range(blocks):
        each(lambda mask: home(block, mask, True).wait_recv())
    load_time.wait()
    width_block = math.gcd(model_width, 512)

    def time_columns(index, carry):
        at = pl.ds(pl.multiple_of(index * width_block, width_block), width_block)
        stream[:, at] = patches[:, at].astype(F32) + jnp.dot(
            mixed[...], w_time[:, at], preferred_element_type=F32
        )
        return carry

    lax.fori_loop(0, model_width // width_block, time_columns, 0)
    norm_rows(stream, gain_space, rows)

    load_own.wait()
    own_shard.wait_recv()
    for mask, quarter in arrivals:
        pair(mask, quarter, half, 0).wait_recv()
        pair(mask, quarter, 1 - half, 1).wait_recv()

    project_block = math.gcd(3 * model_width, 512)

    def project(index, carry):
        at = pl.ds(pl.multiple_of(index * project_block, project_block), project_block)
        projected[:, at] = lax.dot_general(
            rows[...], shards_in[at, :], (((1,), (1,)), ((), ())), preferred_element_type=F32
        ).astype(BF16)
        return carry

    lax.fori_loop(0, 3 * model_width // project_block, project, 0)

    def space_heads(index, carry):
        def at(which):
            return pl.ds(pl.multiple_of(which * model_width + index * 128, 128), 128)

        mixed[:, at(0)] = attend(
            projected[:, at(0)], projected[:, at(1)], projected[:, at(2)], head_size, None
        )
        return carry

    lax.fori_loop(0, model_width // 128, space_heads, 0, unroll=6)
    load_merge.wait()

    def merge_columns(index, carry):
        at = pl.ds(pl.multiple_of(index * width_block, width_block), width_block)
        residual[:, at] = stream[:, at] + jnp.dot(
            mixed[...], w_merge[:, at], preferred_element_type=F32
        )
        return carry

    lax.fori_loop(0, model_width // width_block, merge_columns, 0)
    norm_rows(residual, gain_mix, rows)

    def leave(index, carry):
        at = pl.ds(pl.multiple_of(index * width_block, width_block), width_block)
        found = jnp.dot(chosen[...], rows[:, at], preferred_element_type=F32).astype(BF16)
        sent[:, :, at] = found.reshape(EXPERTS, base, width_block)
        return carry

    lax.fori_loop(0, model_width // width_block, leave, 0)
    packed = jnp.zeros((EXPERTS * base, piece_width), F32)
    for piece in range(pieces):
        found = jnp.dot(
            beside[...],
            rows[:, piece * piece_width : (piece + 1) * piece_width],
            preferred_element_type=F32,
        ).astype(BF16)
        packed = packed + jnp.dot(
            piece_rows(EXPERTS, base, extra, pieces, piece, True), found, preferred_element_type=F32
        )
    sent[:, :, model_width:] = packed.astype(BF16).reshape(EXPERTS, base, piece_width)

    for block in range(blocks):
        for array in range(3):
            each(lambda mask: part_out(array, block, mask).wait_send())
        each(lambda mask: home(block, mask, False).wait_send())
    own_shard.wait_send()
    for mask, quarter in arrivals:
        flat(mask, quarter).wait_send()
        deep(mask, quarter, half).wait_send()
        pair(mask, quarter, half, 0).wait_send()
        pair(mask, quarter, 1 - half, 1).wait_send()


def front(
    clip_lengths,
    temporal_q,
    temporal_k,
    temporal_v,
    patches,
    w_time,
    gain_space,
    w_space,
    w_merge,
    gain_mix,
    ids,
):
    frames, clips = lax.axis_size("frame"), lax.axis_size("expert")
    row_count, model_width = patches.shape
    places = row_count // frames
    block_rows = math.gcd(places, 16)
    blocks = places // block_rows
    shard_width = w_space.shape[0]
    base, extra, _, piece_width = slot_layout(model_width)
    vmem = pl.BlockSpec(memory_space=pltpu.VMEM)
    hbm = pl.BlockSpec(memory_space=pl.ANY)
    dma = pltpu.SemaphoreType.DMA
    tube = pltpu.VMEM((blocks, frames, block_rows, model_width), BF16)
    square = pltpu.VMEM((model_width, model_width), BF16)
    others = frames // 2 - 1
    quarters = 2
    return pl.pallas_call(
        functools.partial(front_kernel, frames, clips),
        out_shape=(
            jax.ShapeDtypeStruct((EXPERTS, base, model_width + piece_width), BF16),
            jax.ShapeDtypeStruct((row_count, model_width), F32),
        ),
        in_specs=[
            pl.BlockSpec(memory_space=pltpu.SMEM),
            hbm,
            hbm,
            hbm,
            vmem,
            hbm,
            vmem,
            hbm,
            hbm,
            vmem,
            vmem,
        ],
        out_specs=(vmem, vmem),
        scratch_shapes=[
            tube,
            tube,
            tube,
            tube,
            pltpu.VMEM((row_count, model_width), BF16),
            square,
            square,
            pltpu.VMEM((frames * shard_width, model_width), BF16),
            pltpu.VMEM((row_count, 3 * model_width), BF16),
            pltpu.VMEM((row_count, model_width), F32),
            pltpu.VMEM((row_count, model_width), BF16),
            pltpu.VMEM((EXPERTS * base, row_count), BF16),
            pltpu.VMEM((EXPERTS * extra, row_count), BF16),
            dma((3,)),
            dma((3, blocks)),
            dma((3, blocks, frames)),
            dma((3, blocks, frames)),
            dma((blocks, frames)),
            dma((blocks, frames)),
            dma((others, quarters)),
            dma((others, quarters)),
            dma((others, quarters)),
            dma((others, quarters)),
            dma((others, 2, quarters)),
            dma((others, 2, quarters)),
            dma((2,)),
        ],
        compiler_params=pltpu.CompilerParams(
            collective_id=0, has_side_effects=True, vmem_limit_bytes=60 * 2**20
        ),
        cost_estimate=pl.CostEstimate(
            flops=10 * row_count * model_width * model_width,
            bytes_accessed=10 * model_width * model_width,
            transcendentals=0,
        ),
    )(
        clip_lengths,
        temporal_q,
        temporal_k,
        temporal_v,
        patches,
        w_time,
        gain_space,
        w_space,
        w_merge,
        gain_mix,
        ids,
    )


def expert_kernel(
    frames,
    clips,
    shards_of,
    sent,
    residual,
    ids_ref,
    gate_ref,
    expand_hbm,
    reduce_hbm,
    out_ref,
    expand,
    reduce,
    arrived,
    result,
    back,
    rows,
    hidden,
    spare,
    spread,
    gates_high,
    gates_low,
    weight_sem,
    send_sem,
    arrive_sem,
    return_sem,
    back_sem,
    own_sem,
):
    model_width = out_ref.shape[1]
    row_count = out_ref.shape[0]
    units = expand.shape[1]
    base, extra, pieces, piece_width = slot_layout(model_width)
    devices = frames * clips
    frame, clip = lax.axis_index("frame"), lax.axis_index("expert")
    me = frame * clips + clip
    near, far = range(clips // 2), range(clips // 2, clips)
    order = [mask for both in zip(far, near) for mask in both]
    turns = [(order.index(mask), mask) for both in zip(near, far) for mask in both]

    barrier = pltpu.get_barrier_semaphore()

    def partner(place, mask):
        return flip(frame, place, frames), flip(clip, mask, clips)

    for mask in order:

        def greet(place, carry, mask=mask):
            pl.semaphore_signal(
                barrier, inc=1, device_id=partner(place, mask), device_id_type=MESH
            )
            return carry

        lax.fori_loop(0 if mask else 1, frames, greet, 0)

    parts = weight_sem.shape[1]
    loads = []
    for array, (source, target) in enumerate(((expand_hbm, expand), (reduce_hbm, reduce))):
        step = target.shape[0] // parts
        for part in range(parts):
            span = pl.ds(part * step, step)
            loads.append(
                pltpu.make_async_copy(
                    source.at[0, span], target.at[span], weight_sem.at[array, part]
                )
            )
    for load in loads:
        load.start()
    pl.semaphore_wait(barrier, devices - 1)

    def outward(stage, mask, place):
        there = partner(place, mask)
        expert = lax.div(there[0] * clips + there[1], jnp.int32(shards_of))
        return pltpu.make_async_remote_copy(
            src_ref=sent.at[expert],
            dst_ref=arrived.at[stage, place],
            send_sem=send_sem.at[stage, place],
            recv_sem=arrive_sem.at[stage, place],
            device_id=there,
            device_id_type=MESH,
        )

    def homeward(stage, mask, place):
        return pltpu.make_async_remote_copy(
            src_ref=result.at[stage, place],
            dst_ref=back.at[me],
            send_sem=return_sem.at[stage, place],
            recv_sem=back_sem.at[me],
            device_id=partner(place, mask),
            device_id_type=MESH,
        )

    def over(mask, action):
        def step(place, carry):
            action(place)
            return carry

        lax.fori_loop(0 if mask else 1, frames, step, 0)

    for stage, mask in enumerate(order):
        over(mask, lambda place: outward(stage, mask, place).start())
    own_stage = order.index(0)
    own_in = pltpu.make_async_copy(
        sent.at[lax.div(me, jnp.int32(shards_of))], arrived.at[own_stage, 0], own_sem.at[0]
    )
    own_in.start()

    first, second = slot_rows(ids_ref, devices, shards_of, base, extra)
    gates = jnp.where(first, gate_ref[0:1, :], jnp.where(second, gate_ref[1:2, :], 0.0))
    for at in (slice(0, devices * base), slice(devices * base, devices * (base + extra))):
        turned = gates[at].T
        high = turned.astype(BF16)
        gates_high[:, at] = high
        gates_low[:, at] = (turned - high.astype(F32)).astype(BF16)

    group = frames * base
    unit_block = math.gcd(units, 512)
    width_block = math.gcd(model_width, 512)
    for turn, (stage, mask) in enumerate(turns):
        over(mask, lambda place: outward(stage, mask, place).wait_recv())
        if mask == 0:
            own_in.wait()
        if turn == 0:
            for load in loads[:parts]:
                load.wait()
        rows[0:group, :] = arrived[stage, :, :, 0:model_width].reshape(group, model_width)
        beside = arrived[stage, :, :, model_width:].reshape(group, piece_width)
        for piece in range(pieces):
            picker = piece_rows(frames, base, extra, pieces, piece, False)
            rows[group:, piece * piece_width : (piece + 1) * piece_width] = jnp.dot(
                picker, beside, preferred_element_type=F32
            ).astype(BF16)

        def widen(block, carry):
            at = pl.ds(pl.multiple_of(block * unit_block, unit_block), unit_block)
            value = jnp.dot(rows[...], expand[:, at], preferred_element_type=F32)
            value = 0.5 * value * (1.0 + lax.erf(value * math.sqrt(0.5)))
            hidden[:, at] = value.astype(BF16)
            return carry

        lax.fori_loop(0, units // unit_block, widen, 0)
        if turn == 0:
            for load in loads[parts:]:
                load.wait()

        def narrow(block, carry):
            at = pl.ds(pl.multiple_of(block * width_block, width_block), width_block)
            value = jnp.dot(hidden[...], reduce[:, at], preferred_element_type=F32).astype(BF16)
            result[stage, :, :, at] = value[0:group].reshape(frames, base, width_block)
            spare[:, at] = value[group:]
            return carry

        lax.fori_loop(0, model_width // width_block, narrow, 0)
        packed = jnp.zeros((group, piece_width), F32)
        for piece in range(pieces):
            packed = packed + jnp.dot(
                piece_rows(frames, base, extra, pieces, piece, True),
                spare[:, piece * piece_width : (piece + 1) * piece_width],
                preferred_element_type=F32,
            )
        result[stage, :, :, model_width:] = packed.astype(BF16).reshape(frames, base, piece_width)
        over(mask, lambda place: homeward(stage, mask, place).start())
        if mask == 0:
            own_out = pltpu.make_async_copy(result.at[stage, 0], back.at[me], own_sem.at[1])
            own_out.start()

    for stage, mask in enumerate(order):

        def settle(place, carry, stage=stage, mask=mask):
            outward(stage, mask, place).wait_send()
            homeward(stage, mask, place).wait_send()
            there = partner(place, mask)
            pltpu.make_async_remote_copy(
                src_ref=result.at[stage, place],
                dst_ref=back.at[there[0] * clips + there[1]],
                send_sem=return_sem.at[stage, place],
                recv_sem=back_sem.at[there[0] * clips + there[1]],
                device_id=there,
                device_id_type=MESH,
            ).wait_recv()
            return carry

        lax.fori_loop(0 if mask else 1, frames, settle, 0)
    own_out.wait()

    beside = back[:, :, model_width:].reshape(devices * base, piece_width)
    for piece in range(pieces):
        picker = piece_rows(devices, base, extra, pieces, piece, False)
        spread[:, piece * piece_width : (piece + 1) * piece_width] = jnp.dot(
            picker, beside, preferred_element_type=F32
        ).astype(BF16)

    def mix(block, carry):
        at = pl.ds(pl.multiple_of(block * width_block, width_block), width_block)
        total = residual[:, at]
        main = back[:, :, at].reshape(devices * base, width_block)
        for gate in (gates_high, gates_low):
            total = total + jnp.dot(
                gate[:, 0 : devices * base], main, preferred_element_type=F32
            )
            total = total + jnp.dot(
                gate[:, devices * base :], spread[:, at], preferred_element_type=F32
            )
        out_ref[:, at] = total.astype(BF16)
        return carry

    lax.fori_loop(0, model_width // width_block, mix, 0)


def expert_mix(sent, residual, ids, gates, w_expand, w_reduce):
    frames, clips = lax.axis_size("frame"), lax.axis_size("expert")
    devices = frames * clips
    row_count, model_width = residual.shape
    units = w_expand.shape[2]
    base, extra, _, piece_width = slot_layout(model_width)
    block = (base, model_width + piece_width)
    group = frames * (base + extra)
    columns = devices * (base + extra)
    parts = 4
    vmem = pl.BlockSpec(memory_space=pltpu.VMEM)
    hbm = pl.BlockSpec(memory_space=pl.ANY)
    dma = pltpu.SemaphoreType.DMA
    return pl.pallas_call(
        functools.partial(expert_kernel, frames, clips, devices // EXPERTS),
        out_shape=jax.ShapeDtypeStruct((row_count, model_width), BF16),
        in_specs=[hbm, vmem, vmem, vmem, hbm, hbm],
        out_specs=vmem,
        scratch_shapes=[
            pltpu.VMEM(w_expand.shape[1:], BF16),
            pltpu.VMEM(w_reduce.shape[1:], BF16),
            pltpu.VMEM((clips, frames) + block, BF16),
            pltpu.VMEM((clips, frames) + block, BF16),
            pltpu.VMEM((devices,) + block, BF16),
            pltpu.VMEM((group, model_width), BF16),
            pltpu.VMEM((group, units), BF16),
            pltpu.VMEM((frames * extra, model_width), BF16),
            pltpu.VMEM((devices * extra, model_width), BF16),
            pltpu.VMEM((row_count, columns), BF16),
            pltpu.VMEM((row_count, columns), BF16),
            dma((2, parts)),
            dma((clips, frames)),
            dma((clips, frames)),
            dma((clips, frames)),
            dma((devices,)),
            dma((2,)),
        ],
        compiler_params=pltpu.CompilerParams(
            collective_id=1, has_side_effects=True, vmem_limit_bytes=60 * 2**20
        ),
        cost_estimate=pl.CostEstimate(
            flops=4 * columns * model_width * units,
            bytes_accessed=4 * model_width * units,
            transcendentals=0,
        ),
    )(sent, residual, ids, gates, w_expand, w_reduce)


def shards(
    patches,
    temporal_q,
    temporal_k,
    temporal_v,
    clip_lengths,
    w_time,
    gain_space,
    w_space,
    w_merge,
    gain_mix,
    expert_ids,
    gate_weights,
    w_expand,
    w_reduce,
):
    local_shape = patches.shape
    model_width = local_shape[-1]
    flat = (-1, model_width)
    ids = expert_ids.reshape(-1, 2).T
    sent, residual = front(
        clip_lengths,
        temporal_q.reshape(flat),
        temporal_k.reshape(flat),
        temporal_v.reshape(flat),
        patches.reshape(flat),
        w_time,
        gain_space,
        w_space.T,
        w_merge,
        gain_mix,
        ids,
    )
    mixed = expert_mix(sent, residual, ids, gate_weights.reshape(-1, 2).T, w_expand, w_reduce)
    return mixed.reshape(local_shape)


def solution(mesh):
    return jax.shard_map(
        shards,
        mesh=mesh,
        in_specs=(
            P("frame", "expert", None, None),
            P("frame", "expert", None, None),
            P("frame", "expert", None, None),
            P("frame", "expert", None, None),
            P("expert"),
            P(),
            P(),
            P(None, "frame"),
            P(),
            P(),
            P("frame", "expert", None, None),
            P("frame", "expert", None, None),
            P(("frame", "expert"), None, None),
            P(("frame", "expert"), None, None),
        ),
        out_specs=P("frame", "expert", None, None),
        check_vma=False,
    )
```

```python
import functools
import math

import jax
import jax.numpy as jnp
from jax import lax
from jax.experimental import pallas as pl
from jax.experimental.pallas import tpu as pltpu
from jax.sharding import PartitionSpec as P

HEADS = 24
EXPERTS = 32
CAP = 18


epsilon = 1e-06


def layer_norm(values, gain_vector):
    centre = values - jnp.mean(values, axis=-1, keepdims=True)
    spread = jnp.mean(centre * centre, axis=-1, keepdims=True)
    return (centre * lax.rsqrt(spread + epsilon) * gain_vector).astype(jnp.bfloat16)


MESH = pl.DeviceIdType.MESH
F32, BF16 = jnp.float32, jnp.bfloat16


def flip(index, mask, size):
    total, weight = 0, 1
    while weight < size:
        here = lax.rem(lax.div(index, jnp.int32(weight)), jnp.int32(2))
        there = lax.rem(lax.div(jnp.int32(mask), jnp.int32(weight)), jnp.int32(2))
        total = total + weight * lax.rem(here + there, jnp.int32(2))
        weight *= 2
    return total


def slot_layout(model_width):
    base = CAP // 16 * 16
    extra = CAP - base
    pieces = base // max(extra, 1)
    while model_width % (pieces * 128):
        pieces -= 1
    return base, extra, pieces, model_width // pieces


def piece_rows(group, base, extra, pieces, piece, turned):
    shape = (group * base, group * extra) if turned else (group * extra, group * base)
    slot = lax.broadcasted_iota(jnp.int32, shape, 1 if turned else 0)
    row = lax.broadcasted_iota(jnp.int32, shape, 0 if turned else 1)
    wanted = lax.div(slot, extra) * base + lax.rem(slot, extra) * pieces + piece
    return (row == wanted).astype(F32).astype(BF16)


def norm_rows(source, gain_ref, target):
    row_count = source.shape[0]
    block = math.gcd(row_count, 64)

    def step(index, carry):
        at = pl.ds(pl.multiple_of(index * block, block), block)
        target[at, :] = layer_norm(source[at, :], gain_ref[...].reshape(1, -1))
        return carry

    lax.fori_loop(0, row_count // block, step, 0)


def attend(query, key_rows, value, head_size, valid):
    lane = lax.broadcasted_iota(jnp.int32, query.shape, 1)
    scaled = query * jnp.asarray(head_size**-0.5, query.dtype)
    mixed = None
    for head in range(query.shape[1] // head_size):
        mine = (lane >= head * head_size) & (lane < (head + 1) * head_size)
        scores = lax.dot_general(
            jnp.where(mine, scaled, jnp.zeros_like(scaled)),
            key_rows,
            (((1,), (1,)), ((), ())),
            preferred_element_type=F32,
        )
        if valid is not None:
            scores = jnp.where(valid, scores, -1e30)
        powers = jnp.exp(scores - jnp.max(scores, axis=-1, keepdims=True))
        found = jnp.dot(powers.astype(BF16), value, preferred_element_type=F32)
        found = found * (1.0 / jnp.sum(powers, axis=-1, keepdims=True))
        mixed = found if mixed is None else jnp.where(mine, found, mixed)
    return mixed.astype(BF16)


def slot_rows(ids_ref, owners, shards_of, base, extra):
    row_count = ids_ref.shape[1]
    place = lax.broadcasted_iota(jnp.int32, (owners * (base + extra), 1), 0)
    tail = place - owners * base
    owner = jnp.where(tail < 0, lax.div(place, base), lax.div(tail, extra))
    slot = jnp.where(tail < 0, lax.rem(place, base), base + lax.rem(tail, extra))
    expert = lax.div(owner, shards_of)
    first = ids_ref[0:1, :] == expert
    second = ids_ref[1:2, :] == expert
    named = jnp.where(first | second, 1.0, 0.0)
    above = lax.broadcasted_iota(jnp.int32, (row_count, row_count), 1)
    earlier = (lax.broadcasted_iota(jnp.int32, (row_count, row_count), 0) < above).astype(F32)
    taken = jnp.dot(named.astype(BF16), earlier.astype(BF16), preferred_element_type=F32)
    here = taken == slot.astype(F32)
    return first & here, second & here


def front_kernel(
    frames,
    clips,
    length_ref,
    query_hbm,
    key_hbm,
    value_hbm,
    patches,
    time_hbm,
    gain_space,
    space_hbm,
    merge_hbm,
    gain_mix,
    ids_ref,
    sent,
    residual,
    queries,
    key_rows,
    values,
    tubes,
    mixed,
    w_time,
    w_merge,
    shards_in,
    projected,
    stream,
    rows,
    chosen,
    beside,
    load_sem,
    own_sem,
    part_send,
    part_come,
    home_send,
    home_come,
    flat_send,
    flat_come,
    deep_send,
    deep_come,
    pair_send,
    pair_come,
    whole_sem,
):
    row_count, model_width = residual.shape
    head_size = model_width // HEADS
    blocks, _, block_rows, _ = queries.shape
    places = blocks * block_rows
    base, extra, pieces, piece_width = slot_layout(model_width)
    shard_width = space_hbm.shape[0]
    frame, clip = lax.axis_index("frame"), lax.axis_index("expert")
    half = lax.rem(clip, 2)

    def beside_frame(mask):
        return flip(frame, mask, frames), clip

    partner = (frame, clip + 1 - 2 * half)
    barrier = pltpu.get_barrier_semaphore()

    def greet(mask, carry):
        pl.semaphore_signal(barrier, inc=1, device_id=beside_frame(mask), device_id_type=MESH)
        return carry

    lax.fori_loop(1, frames, greet, 0)
    pl.semaphore_signal(barrier, inc=1, device_id=partner, device_id_type=MESH)

    own_rows = pl.ds(pl.multiple_of(frame * shard_width, 16), shard_width)
    load_own = pltpu.make_async_copy(space_hbm, shards_in.at[own_rows], load_sem.at[0])
    load_time = pltpu.make_async_copy(time_hbm, w_time, load_sem.at[1])
    load_merge = pltpu.make_async_copy(merge_hbm, w_merge, load_sem.at[2])
    pl.semaphore_wait(barrier, frames)

    def remote(source, target, send_sem, come_sem, there):
        return pltpu.make_async_remote_copy(
            src_ref=source,
            dst_ref=target,
            send_sem=send_sem,
            recv_sem=come_sem,
            device_id=there,
            device_id_type=MESH,
        )

    quarters = 2
    evens = range(2, frames, 2)
    place_of = {mask: number for number, mask in enumerate(evens)}

    def way(mask, quarter):
        return mask & -mask if quarter == 0 else 1 << (mask.bit_length() - 1)

    def span(start, quarter, which):
        share = shard_width // 2
        first = -(-share // 32) * 16
        start = start + which * share + (0, first)[quarter]
        return pl.ds(pl.multiple_of(start, 16), (first, share - first)[quarter])

    def shard_of(mask):
        return flip(frame, mask, frames) * shard_width

    def flat(mask, quarter):
        by = way(mask, quarter)
        target = shards_in.at[span(shard_of(mask ^ by), quarter, half)]
        source = target
        if mask == by:
            source = space_hbm.at[span(0, quarter, half)]
        sems = (place_of[mask], quarter)
        return remote(source, target, flat_send.at[sems], flat_come.at[sems], beside_frame(by))

    def deep(mask, quarter, which):
        piece = shards_in.at[span(shard_of(mask), quarter, which)]
        sems = (place_of[mask], quarter)
        return remote(piece, piece, deep_send.at[sems], deep_come.at[sems], partner)

    def pair(mask, quarter, which, number):
        piece = shards_in.at[span(shard_of(mask), quarter, which)]
        sems = (place_of[mask], number, quarter)
        return remote(piece, piece, pair_send.at[sems], pair_come.at[sems], beside_frame(1))

    single = [mask for mask in evens if mask & (mask - 1) == 0]
    double = [mask for mask in evens if mask & (mask - 1)]
    double.sort(key=lambda mask: (bin(mask).count("1"), mask))
    opening = [(mask, 1 if number == 0 else 0) for number, mask in enumerate(single)]
    closing = [
        (mask, quarter)
        for mask in single
        for quarter in range(quarters)
        if (mask, quarter) not in opening
    ]
    for mask, quarter in opening:
        flat(mask, quarter).start()

    arrays = ((query_hbm, queries), (key_hbm, key_rows), (value_hbm, values))

    def part(array, block, mask):
        there = flip(frame, mask, frames)
        source, target = arrays[array]
        start = pl.multiple_of(there * places + block * block_rows, block_rows)
        return source.at[pl.ds(start, block_rows)], target.at[block], there

    def part_out(array, block, mask):
        source, target, there = part(array, block, mask)
        return remote(
            source,
            target.at[frame],
            part_send.at[array, block, mask],
            part_come.at[array, block, mask],
            (there, clip),
        )

    def part_in(array, block, mask):
        source, target, there = part(array, block, mask)
        return remote(
            source,
            target.at[there],
            part_send.at[array, block, mask],
            part_come.at[array, block, mask],
            (there, clip),
        )

    def own_part(array, block):
        source, target, _ = part(array, block, 0)
        return pltpu.make_async_copy(source, target.at[frame], own_sem.at[array, block])

    def each(action):
        def step(mask, carry):
            action(mask)
            return carry

        lax.fori_loop(1, frames, step, 0)

    def send_parts(block):
        for array in range(3):
            each(lambda mask: part_out(array, block, mask).start())
            own_part(array, block).start()

    def home(block, mask, incoming):
        there = flip(frame, mask, frames)
        start = pl.multiple_of(
            (there if incoming else frame) * places + block * block_rows, block_rows
        )
        return remote(
            tubes.at[block, there],
            mixed.at[pl.ds(start, block_rows)],
            home_send.at[block, mask],
            home_come.at[block, mask],
            (there, clip),
        )

    group = frames * block_rows
    row = lax.broadcasted_iota(jnp.int32, (group, group), 0)
    column = lax.broadcasted_iota(jnp.int32, (group, group), 1)
    valid = (lax.rem(row, block_rows) == lax.rem(column, block_rows)) & (
        lax.div(column, block_rows) < length_ref[0]
    )

    def time_block(block):
        for array in range(3):
            each(lambda mask: part_in(array, block, mask).wait_recv())
            own_part(array, block).wait()

        def heads(index, carry):
            at = pl.ds(pl.multiple_of(index * 128, 128), 128)
            found = attend(
                queries[block, :, :, at].reshape(group, 128),
                key_rows[block, :, :, at].reshape(group, 128),
                values[block, :, :, at].reshape(group, 128),
                head_size,
                valid,
            )
            tubes[block, :, :, at] = found.reshape(frames, block_rows, 128)
            return carry

        lax.fori_loop(0, model_width // 128, heads, 0, unroll=6)
        each(lambda mask: home(block, mask, False).start())
        start = pl.multiple_of(frame * places + block * block_rows, block_rows)
        mixed[pl.ds(start, block_rows), :] = tubes[block, frame]

    def pass_on(mask, quarter):
        flat(mask, quarter).wait_recv()
        for later in double:
            if later ^ way(later, quarter) == mask:
                flat(later, quarter).start()
        deep(mask, quarter, half).start()
        pair(mask, quarter, half, 0).start()

    send_parts(0)
    own_shard = remote(
        space_hbm, shards_in.at[own_rows], whole_sem.at[0], whole_sem.at[1], beside_frame(1)
    )
    own_shard.start()
    load_own.start()
    load_time.start()
    load_merge.start()

    for mask, quarter in opening:
        pass_on(mask, quarter)
    for mask, quarter in closing:
        flat(mask, quarter).start()
    for block in range(1, blocks):
        send_parts(block)

    first, second = slot_rows(ids_ref, EXPERTS, 1, base, extra)
    hits = jnp.where(first | second, 1.0, 0.0).astype(BF16)
    chosen[...] = hits[0 : EXPERTS * base]
    beside[...] = hits[EXPERTS * base :]

    time_block(0)
    ready, rest = list(opening), list(closing)
    for mask in double:
        for quarter in range(quarters):
            from_ready = (mask ^ way(mask, quarter), quarter) in ready
            (ready if from_ready else rest).append((mask, quarter))
    arrivals = ready + rest
    for mask, quarter in arrivals[len(opening) :]:
        pass_on(mask, quarter)
    for block in range(1, blocks):
        time_block(block)
    for mask, quarter in arrivals:
        deep(mask, quarter, 1 - half).wait_recv()
        pair(mask, quarter, 1 - half, 1).start()

    for block in range(blocks):
        each(lambda mask: home(block, mask, True).wait_recv())
    load_time.wait()
    width_block = math.gcd(model_width, 512)

    def time_columns(index, carry):
        at = pl.ds(pl.multiple_of(index * width_block, width_block), width_block)
        stream[:, at] = patches[:, at].astype(F32) + jnp.dot(
            mixed[...], w_time[:, at], preferred_element_type=F32
        )
        return carry

    lax.fori_loop(0, model_width // width_block, time_columns, 0, unroll=3)
    norm_rows(stream, gain_space, rows)

    load_own.wait()
    own_shard.wait_recv()
    for mask, quarter in arrivals:
        pair(mask, quarter, half, 0).wait_recv()
        pair(mask, quarter, 1 - half, 1).wait_recv()

    project_block = math.gcd(3 * model_width, 512)

    def project(index, carry):
        at = pl.ds(pl.multiple_of(index * project_block, project_block), project_block)
        projected[:, at] = lax.dot_general(
            rows[...], shards_in[at, :], (((1,), (1,)), ((), ())), preferred_element_type=F32
        ).astype(BF16)
        return carry

    lax.fori_loop(0, 3 * model_width // project_block, project, 0, unroll=3)

    def space_heads(index, carry):
        def at(which):
            return pl.ds(pl.multiple_of(which * model_width + index * 128, 128), 128)

        mixed[:, at(0)] = attend(
            projected[:, at(0)], projected[:, at(1)], projected[:, at(2)], head_size, None
        )
        return carry

    lax.fori_loop(0, model_width // 128, space_heads, 0, unroll=6)
    load_merge.wait()

    def merge_columns(index, carry):
        at = pl.ds(pl.multiple_of(index * width_block, width_block), width_block)
        residual[:, at] = stream[:, at] + jnp.dot(
            mixed[...], w_merge[:, at], preferred_element_type=F32
        )
        return carry

    lax.fori_loop(0, model_width // width_block, merge_columns, 0, unroll=3)
    norm_rows(residual, gain_mix, rows)

    def leave(index, carry):
        at = pl.ds(pl.multiple_of(index * width_block, width_block), width_block)
        found = jnp.dot(chosen[...], rows[:, at], preferred_element_type=F32).astype(BF16)
        sent[:, :, at] = found.reshape(EXPERTS, base, width_block)
        return carry

    lax.fori_loop(0, model_width // width_block, leave, 0, unroll=3)
    packed = jnp.zeros((EXPERTS * base, piece_width), F32)
    for piece in range(pieces):
        found = jnp.dot(
            beside[...],
            rows[:, piece * piece_width : (piece + 1) * piece_width],
            preferred_element_type=F32,
        ).astype(BF16)
        packed = packed + jnp.dot(
            piece_rows(EXPERTS, base, extra, pieces, piece, True), found, preferred_element_type=F32
        )
    sent[:, :, model_width:] = packed.astype(BF16).reshape(EXPERTS, base, piece_width)

    for block in range(blocks):
        for array in range(3):
            each(lambda mask: part_out(array, block, mask).wait_send())
        each(lambda mask: home(block, mask, False).wait_send())
    own_shard.wait_send()
    for mask, quarter in arrivals:
        flat(mask, quarter).wait_send()
        deep(mask, quarter, half).wait_send()
        pair(mask, quarter, half, 0).wait_send()
        pair(mask, quarter, 1 - half, 1).wait_send()


def front(
    clip_lengths,
    temporal_q,
    temporal_k,
    temporal_v,
    patches,
    w_time,
    gain_space,
    w_space,
    w_merge,
    gain_mix,
    ids,
):
    frames, clips = lax.axis_size("frame"), lax.axis_size("expert")
    row_count, model_width = patches.shape
    places = row_count // frames
    block_rows = math.gcd(places, 16)
    blocks = places // block_rows
    shard_width = w_space.shape[0]
    base, extra, _, piece_width = slot_layout(model_width)
    vmem = pl.BlockSpec(memory_space=pltpu.VMEM)
    hbm = pl.BlockSpec(memory_space=pl.ANY)
    dma = pltpu.SemaphoreType.DMA
    tube = pltpu.VMEM((blocks, frames, block_rows, model_width), BF16)
    square = pltpu.VMEM((model_width, model_width), BF16)
    others = frames // 2 - 1
    quarters = 2
    return pl.pallas_call(
        functools.partial(front_kernel, frames, clips),
        out_shape=(
            jax.ShapeDtypeStruct((EXPERTS, base, model_width + piece_width), BF16),
            jax.ShapeDtypeStruct((row_count, model_width), F32),
        ),
        in_specs=[
            pl.BlockSpec(memory_space=pltpu.SMEM),
            hbm,
            hbm,
            hbm,
            vmem,
            hbm,
            vmem,
            hbm,
            hbm,
            vmem,
            vmem,
        ],
        out_specs=(vmem, vmem),
        scratch_shapes=[
            tube,
            tube,
            tube,
            tube,
            pltpu.VMEM((row_count, model_width), BF16),
            square,
            square,
            pltpu.VMEM((frames * shard_width, model_width), BF16),
            pltpu.VMEM((row_count, 3 * model_width), BF16),
            pltpu.VMEM((row_count, model_width), F32),
            pltpu.VMEM((row_count, model_width), BF16),
            pltpu.VMEM((EXPERTS * base, row_count), BF16),
            pltpu.VMEM((EXPERTS * extra, row_count), BF16),
            dma((3,)),
            dma((3, blocks)),
            dma((3, blocks, frames)),
            dma((3, blocks, frames)),
            dma((blocks, frames)),
            dma((blocks, frames)),
            dma((others, quarters)),
            dma((others, quarters)),
            dma((others, quarters)),
            dma((others, quarters)),
            dma((others, 2, quarters)),
            dma((others, 2, quarters)),
            dma((2,)),
        ],
        compiler_params=pltpu.CompilerParams(
            collective_id=0, has_side_effects=True, vmem_limit_bytes=60 * 2**20
        ),
        cost_estimate=pl.CostEstimate(
            flops=10 * row_count * model_width * model_width,
            bytes_accessed=10 * model_width * model_width,
            transcendentals=0,
        ),
    )(
        clip_lengths,
        temporal_q,
        temporal_k,
        temporal_v,
        patches,
        w_time,
        gain_space,
        w_space,
        w_merge,
        gain_mix,
        ids,
    )


def expert_kernel(
    frames,
    clips,
    shards_of,
    sent,
    residual,
    ids_ref,
    gate_ref,
    expand_hbm,
    reduce_hbm,
    out_ref,
    expand,
    reduce,
    arrived,
    result,
    back,
    rows,
    hidden,
    spare,
    spread,
    gates_high,
    gates_low,
    weight_sem,
    send_sem,
    arrive_sem,
    return_sem,
    back_sem,
    own_sem,
):
    model_width = out_ref.shape[1]
    row_count = out_ref.shape[0]
    units = expand.shape[1]
    base, extra, pieces, piece_width = slot_layout(model_width)
    devices = frames * clips
    frame, clip = lax.axis_index("frame"), lax.axis_index("expert")
    me = frame * clips + clip
    near, far = range(clips // 2), range(clips // 2, clips)
    order = [mask for both in zip(far, near) for mask in both]
    turns = [(order.index(mask), mask) for both in zip(near, far) for mask in both]

    barrier = pltpu.get_barrier_semaphore()

    def partner(place, mask):
        return flip(frame, place, frames), flip(clip, mask, clips)

    for mask in order:

        def greet(place, carry, mask=mask):
            pl.semaphore_signal(
                barrier, inc=1, device_id=partner(place, mask), device_id_type=MESH
            )
            return carry

        lax.fori_loop(0 if mask else 1, frames, greet, 0)

    parts = weight_sem.shape[1]
    loads = []
    for array, (source, target) in enumerate(((expand_hbm, expand), (reduce_hbm, reduce))):
        step = target.shape[0] // parts
        for part in range(parts):
            span = pl.ds(part * step, step)
            loads.append(
                pltpu.make_async_copy(
                    source.at[0, span], target.at[span], weight_sem.at[array, part]
                )
            )
    for load in loads:
        load.start()
    pl.semaphore_wait(barrier, devices - 1)

    def outward(stage, mask, place):
        there = partner(place, mask)
        expert = lax.div(there[0] * clips + there[1], jnp.int32(shards_of))
        return pltpu.make_async_remote_copy(
            src_ref=sent.at[expert],
            dst_ref=arrived.at[stage, place],
            send_sem=send_sem.at[stage, place],
            recv_sem=arrive_sem.at[stage, place],
            device_id=there,
            device_id_type=MESH,
        )

    def homeward(stage, mask, place):
        return pltpu.make_async_remote_copy(
            src_ref=result.at[stage, place],
            dst_ref=back.at[me],
            send_sem=return_sem.at[stage, place],
            recv_sem=back_sem.at[me],
            device_id=partner(place, mask),
            device_id_type=MESH,
        )

    def over(mask, action):
        def step(place, carry):
            action(place)
            return carry

        lax.fori_loop(0 if mask else 1, frames, step, 0)

    for stage, mask in enumerate(order):
        over(mask, lambda place: outward(stage, mask, place).start())
    own_stage = order.index(0)
    own_in = pltpu.make_async_copy(
        sent.at[lax.div(me, jnp.int32(shards_of))], arrived.at[own_stage, 0], own_sem.at[0]
    )
    own_in.start()

    first, second = slot_rows(ids_ref, devices, shards_of, base, extra)
    gates = jnp.where(first, gate_ref[0:1, :], jnp.where(second, gate_ref[1:2, :], 0.0))
    for at in (slice(0, devices * base), slice(devices * base, devices * (base + extra))):
        turned = gates[at].T
        high = turned.astype(BF16)
        gates_high[:, at] = high
        gates_low[:, at] = (turned - high.astype(F32)).astype(BF16)

    group = frames * base
    unit_block = math.gcd(units, 512)
    width_block = math.gcd(model_width, 512)
    for turn, (stage, mask) in enumerate(turns):
        over(mask, lambda place: outward(stage, mask, place).wait_recv())
        if mask == 0:
            own_in.wait()
        if turn == 0:
            for load in loads[:parts]:
                load.wait()
        rows[0:group, :] = arrived[stage, :, :, 0:model_width].reshape(group, model_width)
        beside = arrived[stage, :, :, model_width:].reshape(group, piece_width)
        for piece in range(pieces):
            picker = piece_rows(frames, base, extra, pieces, piece, False)
            rows[group:, piece * piece_width : (piece + 1) * piece_width] = jnp.dot(
                picker, beside, preferred_element_type=F32
            ).astype(BF16)

        def widen(block, carry):
            at = pl.ds(pl.multiple_of(block * unit_block, unit_block), unit_block)
            value = jnp.dot(rows[...], expand[:, at], preferred_element_type=F32)
            value = 0.5 * value * (1.0 + lax.erf(value * math.sqrt(0.5)))
            hidden[:, at] = value.astype(BF16)
            return carry

        lax.fori_loop(0, units // unit_block, widen, 0, unroll=3)
        if turn == 0:
            for load in loads[parts:]:
                load.wait()

        def narrow(block, carry):
            at = pl.ds(pl.multiple_of(block * width_block, width_block), width_block)
            value = jnp.dot(hidden[...], reduce[:, at], preferred_element_type=F32).astype(BF16)
            result[stage, :, :, at] = value[0:group].reshape(frames, base, width_block)
            spare[:, at] = value[group:]
            return carry

        lax.fori_loop(0, model_width // width_block, narrow, 0, unroll=3)
        packed = jnp.zeros((group, piece_width), F32)
        for piece in range(pieces):
            packed = packed + jnp.dot(
                piece_rows(frames, base, extra, pieces, piece, True),
                spare[:, piece * piece_width : (piece + 1) * piece_width],
                preferred_element_type=F32,
            )
        result[stage, :, :, model_width:] = packed.astype(BF16).reshape(frames, base, piece_width)
        over(mask, lambda place: homeward(stage, mask, place).start())
        if mask == 0:
            own_out = pltpu.make_async_copy(result.at[stage, 0], back.at[me], own_sem.at[1])
            own_out.start()

    for stage, mask in enumerate(order):

        def settle(place, carry, stage=stage, mask=mask):
            outward(stage, mask, place).wait_send()
            homeward(stage, mask, place).wait_send()
            there = partner(place, mask)
            pltpu.make_async_remote_copy(
                src_ref=result.at[stage, place],
                dst_ref=back.at[there[0] * clips + there[1]],
                send_sem=return_sem.at[stage, place],
                recv_sem=back_sem.at[there[0] * clips + there[1]],
                device_id=there,
                device_id_type=MESH,
            ).wait_recv()
            return carry

        lax.fori_loop(0 if mask else 1, frames, settle, 0)
    own_out.wait()

    beside = back[:, :, model_width:].reshape(devices * base, piece_width)
    for piece in range(pieces):
        picker = piece_rows(devices, base, extra, pieces, piece, False)
        spread[:, piece * piece_width : (piece + 1) * piece_width] = jnp.dot(
            picker, beside, preferred_element_type=F32
        ).astype(BF16)

    def mix(block, carry):
        at = pl.ds(pl.multiple_of(block * width_block, width_block), width_block)
        total = residual[:, at]
        main = back[:, :, at].reshape(devices * base, width_block)
        for gate in (gates_high, gates_low):
            total = total + jnp.dot(
                gate[:, 0 : devices * base], main, preferred_element_type=F32
            )
            total = total + jnp.dot(
                gate[:, devices * base :], spread[:, at], preferred_element_type=F32
            )
        out_ref[:, at] = total.astype(BF16)
        return carry

    lax.fori_loop(0, model_width // width_block, mix, 0, unroll=3)


def expert_mix(sent, residual, ids, gates, w_expand, w_reduce):
    frames, clips = lax.axis_size("frame"), lax.axis_size("expert")
    devices = frames * clips
    row_count, model_width = residual.shape
    units = w_expand.shape[2]
    base, extra, _, piece_width = slot_layout(model_width)
    block = (base, model_width + piece_width)
    group = frames * (base + extra)
    columns = devices * (base + extra)
    parts = 4
    vmem = pl.BlockSpec(memory_space=pltpu.VMEM)
    hbm = pl.BlockSpec(memory_space=pl.ANY)
    dma = pltpu.SemaphoreType.DMA
    return pl.pallas_call(
        functools.partial(expert_kernel, frames, clips, devices // EXPERTS),
        out_shape=jax.ShapeDtypeStruct((row_count, model_width), BF16),
        in_specs=[hbm, vmem, vmem, vmem, hbm, hbm],
        out_specs=vmem,
        scratch_shapes=[
            pltpu.VMEM(w_expand.shape[1:], BF16),
            pltpu.VMEM(w_reduce.shape[1:], BF16),
            pltpu.VMEM((clips, frames) + block, BF16),
            pltpu.VMEM((clips, frames) + block, BF16),
            pltpu.VMEM((devices,) + block, BF16),
            pltpu.VMEM((group, model_width), BF16),
            pltpu.VMEM((group, units), BF16),
            pltpu.VMEM((frames * extra, model_width), BF16),
            pltpu.VMEM((devices * extra, model_width), BF16),
            pltpu.VMEM((row_count, columns), BF16),
            pltpu.VMEM((row_count, columns), BF16),
            dma((2, parts)),
            dma((clips, frames)),
            dma((clips, frames)),
            dma((clips, frames)),
            dma((devices,)),
            dma((2,)),
        ],
        compiler_params=pltpu.CompilerParams(
            collective_id=1, has_side_effects=True, vmem_limit_bytes=60 * 2**20
        ),
        cost_estimate=pl.CostEstimate(
            flops=4 * columns * model_width * units,
            bytes_accessed=4 * model_width * units,
            transcendentals=0,
        ),
    )(sent, residual, ids, gates, w_expand, w_reduce)


def shards(
    patches,
    temporal_q,
    temporal_k,
    temporal_v,
    clip_lengths,
    w_time,
    gain_space,
    w_space,
    w_merge,
    gain_mix,
    expert_ids,
    gate_weights,
    w_expand,
    w_reduce,
):
    local_shape = patches.shape
    model_width = local_shape[-1]
    flat = (-1, model_width)
    ids = expert_ids.reshape(-1, 2).T
    sent, residual = front(
        clip_lengths,
        temporal_q.reshape(flat),
        temporal_k.reshape(flat),
        temporal_v.reshape(flat),
        patches.reshape(flat),
        w_time,
        gain_space,
        w_space.T,
        w_merge,
        gain_mix,
        ids,
    )
    mixed = expert_mix(sent, residual, ids, gate_weights.reshape(-1, 2).T, w_expand, w_reduce)
    return mixed.reshape(local_shape)


def solution(mesh):
    return jax.shard_map(
        shards,
        mesh=mesh,
        in_specs=(
            P("frame", "expert", None, None),
            P("frame", "expert", None, None),
            P("frame", "expert", None, None),
            P("frame", "expert", None, None),
            P("expert"),
            P(),
            P(),
            P(None, "frame"),
            P(),
            P(),
            P("frame", "expert", None, None),
            P("frame", "expert", None, None),
            P(("frame", "expert"), None, None),
            P(("frame", "expert"), None, None),
        ),
        out_specs=P("frame", "expert", None, None),
        check_vma=False,
    )
```
